512 devices in a mesh: seq: 16 (over x, y_hi, core), shard: 32 (over y_lo, z).
Axes of the slice: x: 4, y: 4 (y_hi: 2, y_lo: 2; y = y_hi * 2 + y_lo), z: 16, core: 2. Of those that a mesh axis runs over, the one named last changes fastest.
Arguments:
- features: bfloat16 [4096, 4096], P('seq', 'shard'), may hold values from -6 to 6
- in_proj: bfloat16 [4096, 3, 4096], P(None, None, 'shard'), may hold values from -0.09375 to 0.09375
- short_filter: float32 [3, 3, 4096], replicated, may hold values from -3.5 to 3.5
- residue: float32 [16, 4096], P(None, 'shard'), may hold values from -1.5 to 1.5
- decay_rate: float32 [16, 4096], P(None, 'shard'), may hold values from 0.05 to 1000
- skip_gain: float32 [4096], P('shard'), may hold values from -4 to 4
Outputs:
- gated: bfloat16 [4096, 4096], P('seq', 'shard')
The draws below stay inside these ranges and needn't reach their ends.
All inputs are finite; a program needn't handle non-finite values.
Results may differ from the reference program's by a relative error of at most 0.0063.
Values may be sent and summed in bfloat16 or wider, within the bound.
No kernel may reach another device: no remote copies, remote signals or barrier semaphores. Data moves between devices by JAX's collectives and lax.ppermute only.
A program may use at most 64 MiB of HBM per device.

```python
import math
import jax
import jax.numpy as jnp
from jax import lax

D = 4096
MODES = 16
TAPS = 3
WINDOW = 4096


def levels(rng, extent, shards, least, top_value):
    level = 1.0
    for axis_at, shards_of in shards:
        draws = jax.random.uniform(jax.random.fold_in(jax.random.fold_in(rng, 6), axis_at), (shards_of,), jnp.float32, least / len(shards), top_value / len(shards))
        level = level * jnp.repeat(jnp.exp(draws), extent[axis_at] // shards_of).reshape((-1,) + (1,) * (len(extent) - 1 - axis_at))
    return level


def gaussian(stream_key, extent, scale, limit, cuts=(), held_as=jnp.bfloat16):
    result = jax.random.normal(stream_key, extent, jnp.float32) * scale
    if len(cuts) > 0:
        result = levels(stream_key, extent, cuts, -0.22, 0.18) * result
    return jnp.clip(result, min=-limit, max=limit).astype(held_as)


def setup_inputs(seed: int = 0) -> dict:
    keys = jax.random.split(jax.random.key(seed), 7)
    features = gaussian(keys[0], (WINDOW, D), 1.0, 6.0, ((0, 16), (1, 32)))
    in_proj = gaussian(keys[1], (D, 3, D), D ** -0.5, 0.09375, ((2, 32),))
    short_filter = gaussian(keys[2], (TAPS, 3, D), TAPS ** -0.5, 3.5, (), jnp.float32)
    residue = gaussian(keys[3], (MODES, D), 0.25, 1.5, ((1, 32),), jnp.float32)
    decay_rate = jnp.clip(jnp.exp(math.log(1000.0) - 9.9034875 * jax.random.uniform(keys[4], (MODES, D), jnp.float32) ** levels(keys[4], (MODES, D), ((1, 32),), -0.2, 0.2)), 0.05, 1000.0)
    skip_gain = gaussian(keys[5], (D,), 1.0, 4.0, ((0, 32),), jnp.float32)
    return dict(features=features, in_proj=in_proj, short_filter=short_filter, residue=residue, decay_rate=decay_rate, skip_gain=skip_gain)


def mode_tables(residue, decay_rate, total_len, block_len):
    step_rate = decay_rate / total_len
    mode_gain = residue * jnp.sqrt(jnp.expm1(-2.0 * step_rate) / jnp.expm1(-2.0 * decay_rate))
    steps = jnp.arange(block_len, dtype=jnp.float32)[:, None, None]
    lagged = jnp.exp(-step_rate * steps)
    kernel = lax.optimization_barrier(jnp.sum(mode_gain * lagged, axis=1))
    offsets = jnp.arange(block_len)[:, None] - jnp.arange(block_len)[None, :]
    toeplitz = jnp.where((offsets >= 0)[:, :, None], kernel[jnp.clip(offsets, 0, block_len - 1)], 0.0)
    head_table = mode_gain * jnp.exp(-step_rate * (steps + 1.0))
    tail_table = jnp.exp(-step_rate * (block_len - 1.0 - steps))
    step_decay = jnp.exp(-step_rate * block_len)
    return (toeplitz, head_table, tail_table, step_decay)

def reference(features, in_proj, short_filter, residue, decay_rate, skip_gain):
    total_len = features.shape[0]
    model_width = features.shape[1]
    tap_count = short_filter.shape[0]
    proj = jnp.dot(features, in_proj.reshape(model_width, 3 * model_width), preferred_element_type=jnp.float32)
    proj = proj.astype(jnp.bfloat16).reshape(total_len, 3, model_width)
    padded = jnp.concatenate([jnp.zeros((tap_count - 1, 3, model_width), jnp.bfloat16), proj], 0).astype(jnp.float32)
    filtered = jnp.zeros((total_len, 3, model_width), jnp.float32)
    for tap_index in range(tap_count):
        start_row = tap_count - 1 - tap_index
        filtered = filtered + short_filter[tap_index] * padded[start_row:start_row + total_len]
    drive_term = filtered[:, 1, :] * filtered[:, 2, :]
    block_len = math.gcd(total_len, 128)
    block_count = total_len // block_len
    toeplitz, head_table, tail_table, step_decay = mode_tables(residue, decay_rate, total_len, block_len)
    highest = lax.Precision.HIGHEST

    def advance(carried, block_in):
        block_out = jnp.einsum('tsc,sc->tc', toeplitz, block_in, precision=highest)
        block_out = block_out + jnp.einsum('tmc,mc->tc', head_table, carried, precision=highest)
        updated = carried * step_decay + jnp.einsum('sc,smc->mc', block_in, tail_table, precision=highest)
        return (updated, block_out)
    start_state = jnp.zeros(residue.shape, jnp.float32)
    last_state, longconv = lax.scan(advance, start_state, drive_term.reshape(block_count, block_len, model_width))
    longconv = longconv.reshape(total_len, model_width)
    return (filtered[:, 0, :] * (longconv + skip_gain * drive_term)).astype(jnp.bfloat16)
```

```python
import functools

import jax
import jax.numpy as jnp
from jax import lax
from jax.experimental import pallas as pl
from jax.experimental.pallas import tpu as pltpu
from jax.sharding import PartitionSpec as P

TILE = 8
ROWS = 32


def row_tile(ref, row):
    return jnp.broadcast_to(ref[row : row + 1, :], (TILE, ref.shape[1]))


def tables_kernel(modes, length, total, rate_ref, gain_ref, h_ref, e_ref):
    tiles = length // TILE
    step = rate_ref[...] * (1.0 / total)
    lane = jax.lax.broadcasted_iota(jnp.int32, (TILE, step.shape[1]), 0).astype(jnp.float32)
    for q in range(tiles):
        e_ref[q * modes : (q + 1) * modes, :] = jnp.exp(-step * float(TILE * q))
    scaled = [gain_ref[m : m + 1, :] * jnp.exp(-step[m : m + 1, :] * lane) for m in range(modes)]
    for q in range(tiles):
        total_tile = row_tile(e_ref, q * modes) * scaled[0]
        for m in range(1, modes):
            total_tile = total_tile + row_tile(e_ref, q * modes + m) * scaled[m]
        h_ref[q * TILE : (q + 1) * TILE, :] = total_tile


def project_kernel(
    modes, length, total, per_step, x_ref, w_ref, taps_ref, rate_ref, e_ref,
    first_ref, drive_ref, message_ref, acc_ref, proj_ref, filt_ref,
):
    at = pl.program_id(0)
    block = x_ref.shape[2]
    channels = drive_ref.shape[1]

    @pl.when(at == 0)
    def _():
        acc_ref[...] = jnp.zeros_like(acc_ref)

    part = acc_ref[...]
    for i in range(0, per_step, 2):
        left = jnp.concatenate([x_ref[i], x_ref[i + 1]], axis=1)
        part = part + jnp.dot(
            left, w_ref[i * block : (i + 2) * block, :], preferred_element_type=jnp.float32
        )
    acc_ref[...] = part

    @pl.when(at == pl.num_programs(0) - 1)
    def _():
        pad = TILE
        proj_ref[0:pad, :] = jnp.zeros((pad, 3 * channels), jnp.float32)
        proj_ref[pad:, :] = acc_ref[...].astype(jnp.bfloat16).astype(jnp.float32)
        for b in range(3):
            cols = slice(b * channels, (b + 1) * channels)
            value = taps_ref[b : b + 1, :] * proj_ref[pad : pad + length, cols]
            value = value + taps_ref[3 + b : 4 + b, :] * proj_ref[pad - 1 : pad - 1 + length, cols]
            value = value + taps_ref[6 + b : 7 + b, :] * proj_ref[pad - 2 : pad - 2 + length, cols]
            if b == 0:
                first_ref[...] = value
            else:
                filt_ref[b - 1] = value
        drive = filt_ref[0] * filt_ref[1]
        drive_ref[...] = drive
        row = jax.lax.broadcasted_iota(jnp.int32, (TILE, channels), 0)
        lag = (TILE - 1 - row).astype(jnp.float32)
        tiles = length // TILE
        pieces = [drive_ref[q * TILE : (q + 1) * TILE, :] for q in range(tiles)]
        pieces[0] = jnp.where(row < 2, 0.0, pieces[0])
        step = rate_ref[...] * (1.0 / total)
        for m in range(modes):
            state = row_tile(e_ref, (tiles - 1) * modes + m) * pieces[0]
            for q in range(1, tiles):
                state = state + row_tile(e_ref, (tiles - 1 - q) * modes + m) * pieces[q]
            state = state * jnp.exp(-step[m : m + 1, :] * lag)
            message_ref[m : m + 1, :] = jnp.sum(state, axis=0, keepdims=True)
        one, two, three = channels, 2 * channels, 3 * channels
        head, tail = pad, pad + length - 2
        spots = [
            (head, one, two), (head, two, three), (head + 1, one, two), (head + 1, two, three),
            (tail, one, two), (tail, two, three), (tail + 1, one, two), (tail + 1, two, three),
            (tail, 0, one), (tail + 1, 0, one),
        ]
        for k, (r, lo, hi) in enumerate(spots):
            message_ref[modes + k : modes + k + 1, :] = proj_ref[r : r + 1, lo:hi]
        used = modes + len(spots)
        message_ref[used:ROWS, :] = jnp.zeros((ROWS - used, channels), jnp.float32)


def finish_kernel(
    modes, length, total, seq_count, me_ref, all_ref, first_ref, drive_ref, taps_ref, rate_ref,
    gain_ref, skip_ref, h_ref, e_ref, out_ref, pad_ref, lag_ref, conv_ref,
):
    me = me_ref[0]
    channels = drive_ref.shape[1]
    tiles = length // TILE
    step = rate_ref[...] * (1.0 / total)

    def tap(j, b):
        return taps_ref[3 * j + b : 3 * j + b + 1, :]

    def rows(k):
        return all_ref[pl.ds(modes + k, seq_count, stride=ROWS), :]

    order = jax.lax.broadcasted_iota(jnp.int32, (seq_count, channels), 0)

    def before(k):
        return jnp.where(order == 0, 0.0, pltpu.roll(rows(k), 1, 0))

    starts = [None, None]
    for b in (1, 2):
        head0, head1 = rows(b - 1), rows(2 + b - 1)
        rim0, rim1 = before(4 + b - 1), before(6 + b - 1)
        row0 = tap(0, b) * head0 + tap(1, b) * rim1 + tap(2, b) * rim0
        row1 = tap(0, b) * head1 + tap(1, b) * head0 + tap(2, b) * rim1
        starts = [row0, row1] if b == 1 else [starts[0] * row0, starts[1] * row1]
    start0, start1 = starts
    late0 = jnp.exp(-step * float(length - 1))
    late1 = jnp.exp(-step * float(length - 2))
    fade = jnp.exp(-step * float(length))
    incoming = jnp.zeros((modes, channels), jnp.float32)
    for j in range(seq_count):
        state = all_ref[j * ROWS : j * ROWS + modes, :]
        state = state + late0 * start0[j : j + 1, :] + late1 * start1[j : j + 1, :]
        incoming = jnp.where(j < me, incoming * fade + state, incoming)

    row = jax.lax.broadcasted_iota(jnp.int32, (TILE, channels), 0)
    mine0 = jnp.sum(jnp.where(order == me, start0, 0.0), axis=0, keepdims=True)
    mine1 = jnp.sum(jnp.where(order == me, start1, 0.0), axis=0, keepdims=True)
    rim0 = jnp.sum(jnp.where(order == me - 1, rows(8), 0.0), axis=0, keepdims=True)
    rim1 = jnp.sum(jnp.where(order == me - 1, rows(9), 0.0), axis=0, keepdims=True)
    extra0 = tap(1, 0) * rim1 + tap(2, 0) * rim0
    extra1 = tap(2, 0) * rim1

    pad_ref[0:TILE, :] = jnp.zeros((TILE, channels), jnp.float32)
    pad_ref[TILE:, :] = drive_ref[...]
    head = drive_ref[0:TILE, :]
    head = jnp.where(row == 0, mine0, jnp.where(row == 1, mine1, head))
    pad_ref[TILE : 2 * TILE, :] = head
    for j in range(TILE):
        lag_ref[j] = pad_ref[TILE - j : TILE - j + length, :]

    group = 8
    for g in range(tiles // group):
        low = g * group

        def over_lags(j, accs):
            accs = list(accs)
            window = [lag_ref[j, pl.ds((low + i) * TILE, TILE), :] for i in range(group)]
            for p in range(low + group):
                weight = jnp.broadcast_to(h_ref[pl.ds(TILE * p + j, 1), :], (TILE, channels))
                for i in range(group):
                    if low + i - p >= 0:
                        accs[i] = accs[i] + weight * window[i]
                below = low - p - 1
                fresh = lag_ref[j, pl.ds(below * TILE, TILE), :] if below >= 0 else None
                window = [fresh] + window[:-1]
            return tuple(accs)

        zero = jnp.zeros((TILE, channels), jnp.float32)
        accs = lax.fori_loop(0, TILE, over_lags, (zero,) * group)
        for i in range(group):
            conv_ref[(low + i) * TILE : (low + i + 1) * TILE, :] = accs[i]

    lead = (row + 1).astype(jnp.float32)
    heads = []
    for m in range(modes):
        scale = gain_ref[m : m + 1, :] * incoming[m : m + 1, :]
        heads.append(scale * jnp.exp(-step[m : m + 1, :] * lead))
    skip = skip_ref[...]
    for q in range(tiles):
        at = slice(q * TILE, (q + 1) * TILE)
        value = conv_ref[at, :] + skip * pad_ref[(q + 1) * TILE : (q + 2) * TILE, :]
        for m in range(modes):
            value = value + row_tile(e_ref, q * modes + m) * heads[m]
        gate = first_ref[at, :]
        if q == 0:
            gate = gate + jnp.where(row == 0, extra0, jnp.where(row == 1, extra1, 0.0))
        conv_ref[at, :] = gate * value
    out_ref[...] = conv_ref[...].astype(out_ref.dtype)


def gather_features(features):
    return lax.all_gather(features, "shard", axis=0)


def shards(features, in_proj, short_filter, residue, decay_rate, skip_gain):
    length = features.shape[0]
    channels = in_proj.shape[2]
    modes = residue.shape[0]
    seq_count = lax.axis_size("seq")
    shard_count = lax.axis_size("shard")
    total = length * seq_count
    tiles = length // TILE
    f32 = jnp.float32
    params = pltpu.CompilerParams(vmem_limit_bytes=48 << 20)

    gathered = gather_features(features)
    w_flat = in_proj.reshape(in_proj.shape[0], 3 * channels)
    taps = lax.dynamic_slice_in_dim(
        short_filter, lax.axis_index("shard") * channels, channels, 2
    ).reshape(-1, channels)
    step_rate = decay_rate / total
    gain = residue * jnp.sqrt(jnp.expm1(-2.0 * step_rate) / jnp.expm1(-2.0 * decay_rate))
    h, e = pl.pallas_call(
        functools.partial(tables_kernel, modes, length, total),
        out_shape=(
            jax.ShapeDtypeStruct((length, channels), f32),
            jax.ShapeDtypeStruct((tiles * modes, channels), f32),
        ),
        compiler_params=params,
        name="tables",
    )(decay_rate, gain)

    per_step = 4
    block = features.shape[1]
    whole = lambda shape: pl.BlockSpec(shape, lambda i: (0,) * len(shape))
    first, drive, message = pl.pallas_call(
        functools.partial(project_kernel, modes, length, total, per_step),
        grid=(shard_count // per_step,),
        in_specs=[
            pl.BlockSpec((per_step, length, block), lambda i: (i, 0, 0)),
            pl.BlockSpec((per_step * block, 3 * channels), lambda i: (i, 0)),
            whole(taps.shape),
            whole(decay_rate.shape),
            whole(e.shape),
        ],
        out_specs=(whole((length, channels)), whole((length, channels)), whole((ROWS, channels))),
        out_shape=(
            jax.ShapeDtypeStruct((length, channels), f32),
            jax.ShapeDtypeStruct((length, channels), f32),
            jax.ShapeDtypeStruct((ROWS, channels), f32),
        ),
        scratch_shapes=[
            pltpu.VMEM((length, 3 * channels), f32),
            pltpu.VMEM((length + TILE, 3 * channels), f32),
            pltpu.VMEM((2, length, channels), f32),
        ],
        compiler_params=params,
        name="project",
    )(gathered, w_flat, taps, decay_rate, e)

    spread = jnp.broadcast_to(message[None], (seq_count,) + message.shape)
    everyone = lax.all_to_all(spread, "seq", 0, 0).reshape(seq_count * ROWS, channels)

    me = lax.axis_index("seq").astype(jnp.int32).reshape(1)
    vmem = pl.BlockSpec(memory_space=pltpu.VMEM)
    return pl.pallas_call(
        functools.partial(finish_kernel, modes, length, total, seq_count),
        in_specs=[pl.BlockSpec(memory_space=pltpu.SMEM)] + [vmem] * 9,
        out_specs=vmem,
        out_shape=jax.ShapeDtypeStruct((length, channels), features.dtype),
        scratch_shapes=[
            pltpu.VMEM((length + TILE, channels), f32),
            pltpu.VMEM((TILE, length, channels), f32),
            pltpu.VMEM((length, channels), f32),
        ],
        compiler_params=params,
        name="finish",
    )(me, everyone, first, drive, taps, decay_rate, gain, skip_gain.reshape(1, channels), h, e)


def solution(mesh):
    placed = (
        P("seq", "shard"),
        P(None, None, "shard"),
        P(),
        P(None, "shard"),
        P(None, "shard"),
        P("shard"),
    )
    return jax.shard_map(
        shards, mesh=mesh, in_specs=placed, out_specs=P("seq", "shard"), check_vma=False
    )
```

```python
import functools

import jax
import jax.numpy as jnp
from jax import lax
from jax.experimental import pallas as pl
from jax.experimental.pallas import tpu as pltpu
from jax.sharding import PartitionSpec as P

TILE = 8
ROWS = 32


def row_tile(ref, row):
    return jnp.broadcast_to(ref[row : row + 1, :], (TILE, ref.shape[1]))


def tables_kernel(modes, length, total, rate_ref, gain_ref, h_ref, e_ref):
    tiles = length // TILE
    step = rate_ref[...] * (1.0 / total)
    lane = jax.lax.broadcasted_iota(jnp.int32, (TILE, step.shape[1]), 0).astype(jnp.float32)
    for q in range(tiles):
        e_ref[q * modes : (q + 1) * modes, :] = jnp.exp(-step * float(TILE * q))
    scaled = [gain_ref[m : m + 1, :] * jnp.exp(-step[m : m + 1, :] * lane) for m in range(modes)]
    for q in range(tiles):
        total_tile = row_tile(e_ref, q * modes) * scaled[0]
        for m in range(1, modes):
            total_tile = total_tile + row_tile(e_ref, q * modes + m) * scaled[m]
        h_ref[q * TILE : (q + 1) * TILE, :] = total_tile


def project_kernel(
    modes, length, total, place_ref, near_ref, near_up_ref, near_down_ref, far_ref, far_up_ref,
    far_down_ref, w_ref, taps_ref, rate_ref, e_ref,
    first_ref, drive_ref, message_ref, acc_ref, proj_ref, filt_ref, state_ref,
):
    line, parity = place_ref[0], place_ref[1]
    pairs, _, block = near_ref.shape
    channels = drive_ref.shape[1]
    split = near_up_ref.shape[0]

    def weight(owner):
        at = pl.ds(pl.multiple_of(owner * block, block), block)
        return jnp.concatenate([w_ref[b, at, :] for b in range(3)], axis=1)

    for k in range(pairs):
        near_odd = near_up_ref[k] if k < split else near_down_ref[k - split]
        far_odd = far_up_ref[k] if k < split else far_down_ref[k - split]
        left = jnp.concatenate([near_ref[k], near_odd, far_ref[k], far_odd], axis=1)
        own, other = 2 * pairs * line + 2 * k, 2 * pairs * (1 - line) + 2 * k
        right = jnp.concatenate(
            [weight(own + parity), weight(own + 1 - parity), weight(other + parity), weight(other + 1 - parity)],
            axis=0,
        )
        part = jnp.dot(left, right, preferred_element_type=jnp.float32)
        acc_ref[...] = part if k == 0 else acc_ref[...] + part

    pad = TILE
    proj_ref[0:pad, :] = jnp.zeros((pad, 3 * channels), jnp.float32)
    proj_ref[pad:, :] = acc_ref[...].astype(jnp.bfloat16).astype(jnp.float32)
    for b in range(3):
        cols = slice(b * channels, (b + 1) * channels)
        value = taps_ref[b : b + 1, :] * proj_ref[pad : pad + length, cols]
        value = value + taps_ref[3 + b : 4 + b, :] * proj_ref[pad - 1 : pad - 1 + length, cols]
        value = value + taps_ref[6 + b : 7 + b, :] * proj_ref[pad - 2 : pad - 2 + length, cols]
        if b == 0:
            first_ref[...] = value
        else:
            filt_ref[b - 1] = value
    drive_ref[...] = filt_ref[0] * filt_ref[1]
    row = jax.lax.broadcasted_iota(jnp.int32, (TILE, channels), 0)
    lag = (TILE - 1 - row).astype(jnp.float32)
    tiles = length // TILE
    pieces = [drive_ref[q * TILE : (q + 1) * TILE, :] for q in range(tiles)]
    pieces[0] = jnp.where(row < 2, 0.0, pieces[0])
    step = rate_ref[...] * (1.0 / total)
    for m in range(modes):
        state = row_tile(e_ref, (tiles - 1) * modes + m) * pieces[0]
        for q in range(1, tiles):
            state = state + row_tile(e_ref, (tiles - 1 - q) * modes + m) * pieces[q]
        state = state * jnp.exp(-step[m : m + 1, :] * lag)
        state_ref[m : m + 1, :] = jnp.sum(state, axis=0, keepdims=True)
    one, two, three = channels, 2 * channels, 3 * channels
    head, tail = pad, pad + length - 2
    spots = [
        (head, one, two), (head, two, three), (head + 1, one, two), (head + 1, two, three),
        (tail, one, two), (tail, two, three), (tail + 1, one, two), (tail + 1, two, three),
        (tail, 0, one), (tail + 1, 0, one),
    ]
    for k, (r, lo, hi) in enumerate(spots):
        state_ref[modes + k : modes + k + 1, :] = proj_ref[r : r + 1, lo:hi]
    used = modes + len(spots)
    state_ref[used:ROWS, :] = jnp.zeros((ROWS - used, channels), jnp.float32)
    for s in range(message_ref.shape[0]):
        message_ref[s] = state_ref[...]


def finish_kernel(
    modes, length, total, seq_count, me_ref, all_ref, first_ref, drive_ref, taps_ref, rate_ref,
    gain_ref, skip_ref, h_ref, e_ref, out_ref, pad_ref, lag_ref, conv_ref,
):
    me = me_ref[0]
    channels = drive_ref.shape[1]
    tiles = length // TILE
    step = rate_ref[...] * (1.0 / total)

    def tap(j, b):
        return taps_ref[3 * j + b : 3 * j + b + 1, :]

    def rows(k):
        return all_ref[pl.ds(modes + k, seq_count, stride=ROWS), :]

    order = jax.lax.broadcasted_iota(jnp.int32, (seq_count, channels), 0)

    def before(k):
        return jnp.where(order == 0, 0.0, pltpu.roll(rows(k), 1, 0))

    starts = [None, None]
    for b in (1, 2):
        head0, head1 = rows(b - 1), rows(2 + b - 1)
        rim0, rim1 = before(4 + b - 1), before(6 + b - 1)
        row0 = tap(0, b) * head0 + tap(1, b) * rim1 + tap(2, b) * rim0
        row1 = tap(0, b) * head1 + tap(1, b) * head0 + tap(2, b) * rim1
        starts = [row0, row1] if b == 1 else [starts[0] * row0, starts[1] * row1]
    start0, start1 = starts
    late0 = jnp.exp(-step * float(length - 1))
    late1 = jnp.exp(-step * float(length - 2))
    fade = jnp.exp(-step * float(length))
    incoming = jnp.zeros((modes, channels), jnp.float32)
    for j in range(seq_count):
        state = all_ref[j * ROWS : j * ROWS + modes, :]
        state = state + late0 * start0[j : j + 1, :] + late1 * start1[j : j + 1, :]
        incoming = jnp.where(j < me, incoming * fade + state, incoming)

    row = jax.lax.broadcasted_iota(jnp.int32, (TILE, channels), 0)
    mine0 = jnp.sum(jnp.where(order == me, start0, 0.0), axis=0, keepdims=True)
    mine1 = jnp.sum(jnp.where(order == me, start1, 0.0), axis=0, keepdims=True)
    rim0 = jnp.sum(jnp.where(order == me - 1, rows(8), 0.0), axis=0, keepdims=True)
    rim1 = jnp.sum(jnp.where(order == me - 1, rows(9), 0.0), axis=0, keepdims=True)
    extra0 = tap(1, 0) * rim1 + tap(2, 0) * rim0
    extra1 = tap(2, 0) * rim1

    pad_ref[0:TILE, :] = jnp.zeros((TILE, channels), jnp.float32)
    pad_ref[TILE:, :] = drive_ref[...]
    head = drive_ref[0:TILE, :]
    head = jnp.where(row == 0, mine0, jnp.where(row == 1, mine1, head))
    pad_ref[TILE : 2 * TILE, :] = head
    for j in range(TILE):
        lag_ref[j] = pad_ref[TILE - j : TILE - j + length, :]

    group = 8
    for g in range(tiles // group):
        low = g * group

        def over_lags(j, accs):
            accs = list(accs)
            window = [lag_ref[j, pl.ds((low + i) * TILE, TILE), :] for i in range(group)]
            for p in range(low + group):
                weight = jnp.broadcast_to(h_ref[pl.ds(TILE * p + j, 1), :], (TILE, channels))
                for i in range(group):
                    if low + i - p >= 0:
                        accs[i] = accs[i] + weight * window[i]
                below = low - p - 1
                fresh = lag_ref[j, pl.ds(below * TILE, TILE), :] if below >= 0 else None
                window = [fresh] + window[:-1]
            return tuple(accs)

        zero = jnp.zeros((TILE, channels), jnp.float32)
        accs = lax.fori_loop(0, TILE, over_lags, (zero,) * group)
        for i in range(group):
            conv_ref[(low + i) * TILE : (low + i + 1) * TILE, :] = accs[i]

    lead = (row + 1).astype(jnp.float32)
    heads = []
    for m in range(modes):
        scale = gain_ref[m : m + 1, :] * incoming[m : m + 1, :]
        heads.append(scale * jnp.exp(-step[m : m + 1, :] * lead))
    skip = skip_ref[...]
    for q in range(tiles):
        at = slice(q * TILE, (q + 1) * TILE)
        value = conv_ref[at, :] + skip * pad_ref[(q + 1) * TILE : (q + 2) * TILE, :]
        for m in range(modes):
            value = value + row_tile(e_ref, q * modes + m) * heads[m]
        gate = first_ref[at, :]
        if q == 0:
            gate = gate + jnp.where(row == 0, extra0, jnp.where(row == 1, extra1, 0.0))
        conv_ref[at, :] = gate * value
    out_ref[...] = conv_ref[...].astype(out_ref.dtype)


def gather_features(features):
    shard_count = lax.axis_size("shard")
    line = shard_count // 2
    pairs = line // 2
    groups = [[l * line + 2 * q + p for q in range(pairs)] for l in range(2) for p in range(2)]
    across = [(i, (i + line) % shard_count) for i in range(shard_count)]
    up = [(l * line + z, l * line + (z - 1) % line) for l in range(2) for z in range(line)]
    down = [(l * line + z, l * line + (z + 1) % line) for l in range(2) for z in range(line)]
    half = pairs // 2

    near = lax.all_gather(features, "shard", axis=0, axis_index_groups=groups)
    far = lax.ppermute(near, "shard", across)
    near_up = lax.ppermute(near[:half], "shard", up)
    near_down = lax.ppermute(near[half:], "shard", down)
    far_up = lax.ppermute(far[:half], "shard", up)
    far_down = lax.ppermute(far[half:], "shard", down)
    return near, near_up, near_down, far, far_up, far_down


def shards(features, in_proj, short_filter, residue, decay_rate, skip_gain):
    length = features.shape[0]
    channels = in_proj.shape[2]
    modes = residue.shape[0]
    seq_count = lax.axis_size("seq")
    line = lax.axis_size("shard") // 2
    total = length * seq_count
    tiles = length // TILE
    f32 = jnp.float32
    vmem = pl.BlockSpec(memory_space=pltpu.VMEM)
    smem = pl.BlockSpec(memory_space=pltpu.SMEM)

    def params(mebibytes):
        return pltpu.CompilerParams(vmem_limit_bytes=mebibytes << 20)

    pieces = gather_features(features)
    w_branch = in_proj.transpose(1, 0, 2)
    at = lax.axis_index("shard")
    taps = lax.dynamic_slice_in_dim(short_filter, at * channels, channels, 2).reshape(-1, channels)
    step_rate = decay_rate / total
    gain = residue * jnp.sqrt(jnp.expm1(-2.0 * step_rate) / jnp.expm1(-2.0 * decay_rate))
    h, e = pl.pallas_call(
        functools.partial(tables_kernel, modes, length, total),
        out_shape=(
            jax.ShapeDtypeStruct((length, channels), f32),
            jax.ShapeDtypeStruct((tiles * modes, channels), f32),
        ),
        compiler_params=params(4),
        name="tables",
    )(decay_rate, gain)

    place = jnp.stack([at // line, at % 2]).astype(jnp.int32)
    first, drive, message = pl.pallas_call(
        functools.partial(project_kernel, modes, length, total),
        in_specs=[smem] + [vmem] * 10,
        out_specs=(vmem,) * 3,
        out_shape=(
            jax.ShapeDtypeStruct((length, channels), f32),
            jax.ShapeDtypeStruct((length, channels), f32),
            jax.ShapeDtypeStruct((seq_count, ROWS, channels), f32),
        ),
        scratch_shapes=[
            pltpu.VMEM((length, 3 * channels), f32),
            pltpu.VMEM((length + TILE, 3 * channels), f32),
            pltpu.VMEM((2, length, channels), f32),
            pltpu.VMEM((ROWS, channels), f32),
        ],
        compiler_params=params(16),
        name="project",
    )(place, *pieces, w_branch, taps, decay_rate, e)

    everyone = lax.all_to_all(message, "seq", 0, 0).reshape(seq_count * ROWS, channels)

    me = lax.axis_index("seq").astype(jnp.int32).reshape(1)
    return pl.pallas_call(
        functools.partial(finish_kernel, modes, length, total, seq_count),
        in_specs=[smem] + [vmem] * 9,
        out_specs=vmem,
        out_shape=jax.ShapeDtypeStruct((length, channels), features.dtype),
        scratch_shapes=[
            pltpu.VMEM((length + TILE, channels), f32),
            pltpu.VMEM((TILE, length, channels), f32),
            pltpu.VMEM((length, channels), f32),
        ],
        compiler_params=params(8),
        name="finish",
    )(me, everyone, first, drive, taps, decay_rate, gain, skip_gain.reshape(1, channels), h, e)


def solution(mesh):
    placed = (
        P("seq", "shard"),
        P(None, None, "shard"),
        P(),
        P(None, "shard"),
        P(None, "shard"),
        P("shard"),
    )
    return jax.shard_map(
        shards, mesh=mesh, in_specs=placed, out_specs=P("seq", "shard"), check_vma=False
    )
```

```python
import functools

import jax
import jax.numpy as jnp
from jax import lax
from jax.experimental import pallas as pl
from jax.experimental.pallas import tpu as pltpu
from jax.sharding import PartitionSpec as P

TILE = 8
ROWS = 32


def row_tile(ref, row):
    return jnp.broadcast_to(ref[row : row + 1, :], (TILE, ref.shape[1]))


def tables_kernel(modes, length, total, rate_ref, gain_ref, h_ref, e_ref):
    tiles = length // TILE
    step = rate_ref[...] * (1.0 / total)
    lane = jax.lax.broadcasted_iota(jnp.int32, (TILE, step.shape[1]), 0).astype(jnp.float32)
    for q in range(tiles):
        e_ref[q * modes : (q + 1) * modes, :] = jnp.exp(-step * float(TILE * q))
    scaled = [gain_ref[m : m + 1, :] * jnp.exp(-step[m : m + 1, :] * lane) for m in range(modes)]
    h_ref[0:TILE, :] = jnp.zeros((TILE, step.shape[1]), jnp.float32)
    for q in range(tiles):
        total_tile = row_tile(e_ref, q * modes) * scaled[0]
        for m in range(1, modes):
            total_tile = total_tile + row_tile(e_ref, q * modes + m) * scaled[m]
        h_ref[(q + 1) * TILE : (q + 2) * TILE, :] = total_tile


def weight_rows(w_ref, owners, block):
    rows = []
    for owner in owners:
        at = pl.ds(pl.multiple_of(owner * block, block), block)
        rows.append(jnp.concatenate([w_ref[b, at, :] for b in range(3)], axis=1))
    return jnp.concatenate(rows, axis=0)


def early_kernel(place_ref, near_ref, near_up_ref, near_down_ref, far_ref, w_ref, acc_ref):
    line, parity = place_ref[0], place_ref[1]
    pairs, _, block = near_ref.shape
    split = near_up_ref.shape[0]
    for k in range(0, pairs, 2):
        lefts, owners = [], []
        for i in (k, k + 1):
            odd = near_up_ref[i] if i < split else near_down_ref[i - split]
            lefts += [near_ref[i], odd, far_ref[i]]
            own, other = 2 * pairs * line + 2 * i, 2 * pairs * (1 - line) + 2 * i
            owners += [own + parity, own + 1 - parity, other + parity]
        part = jnp.dot(
            jnp.concatenate(lefts, axis=1),
            weight_rows(w_ref, owners, block),
            preferred_element_type=jnp.float32,
        )
        acc_ref[...] = part if k == 0 else acc_ref[...] + part


def project_kernel(
    modes, length, total, place_ref, early_ref, far_up_ref, far_down_ref, w_ref, taps_ref, rate_ref,
    e_ref, first_ref, drive_ref, message_ref, proj_ref, filt_ref, state_ref,
):
    line, parity = place_ref[0], place_ref[1]
    split, _, block = far_up_ref.shape
    pairs = 2 * split
    channels = drive_ref.shape[1]
    acc = early_ref[...]
    for ref, start in ((far_up_ref, 0), (far_down_ref, split)):
        owners = [2 * pairs * (1 - line) + 2 * (start + k) + 1 - parity for k in range(split)]
        left = jnp.concatenate([ref[k] for k in range(split)], axis=1)
        acc = acc + jnp.dot(
            left, weight_rows(w_ref, owners, block), preferred_element_type=jnp.float32
        )

    pad = TILE
    proj_ref[0:pad, :] = jnp.zeros((pad, 3 * channels), jnp.float32)
    proj_ref[pad:, :] = acc.astype(jnp.bfloat16).astype(jnp.float32)
    for b in range(3):
        cols = slice(b * channels, (b + 1) * channels)
        value = taps_ref[b : b + 1, :] * proj_ref[pad : pad + length, cols]
        value = value + taps_ref[3 + b : 4 + b, :] * proj_ref[pad - 1 : pad - 1 + length, cols]
        value = value + taps_ref[6 + b : 7 + b, :] * proj_ref[pad - 2 : pad - 2 + length, cols]
        if b == 0:
            first_ref[...] = value
        else:
            filt_ref[b - 1] = value
    drive_ref[...] = filt_ref[0] * filt_ref[1]
    row = jax.lax.broadcasted_iota(jnp.int32, (TILE, channels), 0)
    drive_ref[0:TILE, :] = jnp.where(row < 2, 0.0, drive_ref[0:TILE, :])
    lag = (TILE - 1 - row).astype(jnp.float32)
    tiles = length // TILE
    pieces = [drive_ref[q * TILE : (q + 1) * TILE, :] for q in range(tiles)]
    step = rate_ref[...] * (1.0 / total)
    for m in range(modes):
        state = row_tile(e_ref, (tiles - 1) * modes + m) * pieces[0]
        for q in range(1, tiles):
            state = state + row_tile(e_ref, (tiles - 1 - q) * modes + m) * pieces[q]
        state = state * jnp.exp(-step[m : m + 1, :] * lag)
        state_ref[m : m + 1, :] = jnp.sum(state, axis=0, keepdims=True)
    one, two, three = channels, 2 * channels, 3 * channels
    head, tail = pad, pad + length - 2
    spots = [
        (head, one, two), (head, two, three), (head + 1, one, two), (head + 1, two, three),
        (tail, one, two), (tail, two, three), (tail + 1, one, two), (tail + 1, two, three),
        (tail, 0, one), (tail + 1, 0, one),
    ]
    for k, (r, lo, hi) in enumerate(spots):
        state_ref[modes + k : modes + k + 1, :] = proj_ref[r : r + 1, lo:hi]
    used = modes + len(spots)
    state_ref[used:ROWS, :] = jnp.zeros((ROWS - used, channels), jnp.float32)
    for s in range(message_ref.shape[0]):
        message_ref[s] = state_ref[...]


def conv_kernel(length, drive_ref, h_ref, skip_ref, conv_ref, pad_ref, lag_ref):
    channels = drive_ref.shape[1]
    tiles = length // TILE
    pad_ref[0:TILE, :] = jnp.zeros((TILE, channels), jnp.float32)
    pad_ref[TILE:, :] = drive_ref[...]
    for j in range(TILE):
        lag_ref[j] = pad_ref[TILE - j : TILE - j + length, :]

    group = 8
    for g in range(tiles // group):
        low = g * group

        def over_lags(j, accs):
            accs = list(accs)
            window = [lag_ref[j, pl.ds((low + i) * TILE, TILE), :] for i in range(group)]
            for p in range(low + group):
                weight = jnp.broadcast_to(h_ref[pl.ds(TILE * (p + 1) + j, 1), :], (TILE, channels))
                for i in range(group):
                    if low + i - p >= 0:
                        accs[i] = accs[i] + weight * window[i]
                below = low - p - 1
                fresh = lag_ref[j, pl.ds(below * TILE, TILE), :] if below >= 0 else None
                window = [fresh] + window[:-1]
            return tuple(accs)

        accs = tuple(skip_ref[...] * drive_ref[(low + i) * TILE : (low + i + 1) * TILE, :] for i in range(group))
        accs = lax.fori_loop(0, TILE, over_lags, accs)
        for i in range(group):
            conv_ref[(low + i) * TILE : (low + i + 1) * TILE, :] = accs[i]


def finish_kernel(
    modes, length, total, seq_count, me_ref, all_ref, first_ref, conv_ref, taps_ref, rate_ref,
    gain_ref, skip_ref, h_ref, e_ref, out_ref, value_ref,
):
    me = me_ref[0]
    channels = conv_ref.shape[1]
    tiles = length // TILE
    step = rate_ref[...] * (1.0 / total)

    def tap(j, b):
        return taps_ref[3 * j + b : 3 * j + b + 1, :]

    def rows(k):
        return all_ref[pl.ds(modes + k, seq_count, stride=ROWS), :]

    order = jax.lax.broadcasted_iota(jnp.int32, (seq_count, channels), 0)

    def before(k):
        return jnp.where(order == 0, 0.0, pltpu.roll(rows(k), 1, 0))

    starts = [None, None]
    for b in (1, 2):
        head0, head1 = rows(b - 1), rows(2 + b - 1)
        rim0, rim1 = before(4 + b - 1), before(6 + b - 1)
        row0 = tap(0, b) * head0 + tap(1, b) * rim1 + tap(2, b) * rim0
        row1 = tap(0, b) * head1 + tap(1, b) * head0 + tap(2, b) * rim1
        starts = [row0, row1] if b == 1 else [starts[0] * row0, starts[1] * row1]
    start0, start1 = starts
    late0 = jnp.exp(-step * float(length - 1))
    late1 = jnp.exp(-step * float(length - 2))
    fade = jnp.exp(-step * float(length))
    incoming = jnp.zeros((modes, channels), jnp.float32)
    for j in range(seq_count):
        state = all_ref[j * ROWS : j * ROWS + modes, :]
        state = state + late0 * start0[j : j + 1, :] + late1 * start1[j : j + 1, :]
        incoming = jnp.where(j < me, incoming * fade + state, incoming)

    row = jax.lax.broadcasted_iota(jnp.int32, (TILE, channels), 0)
    mine0 = jnp.sum(jnp.where(order == me, start0, 0.0), axis=0, keepdims=True)
    mine1 = jnp.sum(jnp.where(order == me, start1, 0.0), axis=0, keepdims=True)
    rim0 = jnp.sum(jnp.where(order == me - 1, rows(8), 0.0), axis=0, keepdims=True)
    rim1 = jnp.sum(jnp.where(order == me - 1, rows(9), 0.0), axis=0, keepdims=True)
    extra0 = tap(1, 0) * rim1 + tap(2, 0) * rim0
    extra1 = tap(2, 0) * rim1

    lead = (row + 1).astype(jnp.float32)
    heads = []
    for m in range(modes):
        scale = gain_ref[m : m + 1, :] * incoming[m : m + 1, :]
        heads.append(scale * jnp.exp(-step[m : m + 1, :] * lead))
    skip = skip_ref[...]
    for q in range(tiles):
        at = slice(q * TILE, (q + 1) * TILE)
        value = conv_ref[at, :]
        value = value + mine0 * h_ref[(q + 1) * TILE : (q + 2) * TILE, :]
        value = value + mine1 * h_ref[(q + 1) * TILE - 1 : (q + 2) * TILE - 1, :]
        for m in range(modes):
            value = value + row_tile(e_ref, q * modes + m) * heads[m]
        gate = first_ref[at, :]
        if q == 0:
            value = value + jnp.where(row == 0, skip * mine0, jnp.where(row == 1, skip * mine1, 0.0))
            gate = gate + jnp.where(row == 0, extra0, jnp.where(row == 1, extra1, 0.0))
        value_ref[at, :] = gate * value
    out_ref[...] = value_ref[...].astype(out_ref.dtype)


def gather_features(features):
    shard_count = lax.axis_size("shard")
    line = shard_count // 2
    pairs = line // 2
    groups = [[l * line + 2 * q + p for q in range(pairs)] for l in range(2) for p in range(2)]
    across = [(i, (i + line) % shard_count) for i in range(shard_count)]
    up = [(l * line + z, l * line + (z - 1) % line) for l in range(2) for z in range(line)]
    down = [(l * line + z, l * line + (z + 1) % line) for l in range(2) for z in range(line)]
    half = pairs // 2

    near = lax.all_gather(features, "shard", axis=0, axis_index_groups=groups)
    far = lax.ppermute(near, "shard", across)
    near_up = lax.ppermute(near[:half], "shard", up)
    near_down = lax.ppermute(near[half:], "shard", down)
    far_up = lax.ppermute(far[:half], "shard", up)
    far_down = lax.ppermute(far[half:], "shard", down)
    return near, near_up, near_down, far, far_up, far_down


def shards(features, in_proj, short_filter, residue, decay_rate, skip_gain):
    length = features.shape[0]
    channels = in_proj.shape[2]
    modes = residue.shape[0]
    seq_count = lax.axis_size("seq")
    line = lax.axis_size("shard") // 2
    total = length * seq_count
    tiles = length // TILE
    f32 = jnp.float32
    vmem = pl.BlockSpec(memory_space=pltpu.VMEM)
    smem = pl.BlockSpec(memory_space=pltpu.SMEM)

    def params(mebibytes):
        return pltpu.CompilerParams(vmem_limit_bytes=mebibytes << 20)

    pieces = gather_features(features)
    w_branch = in_proj.transpose(1, 0, 2)
    at = lax.axis_index("shard")
    taps = lax.dynamic_slice_in_dim(short_filter, at * channels, channels, 2).reshape(-1, channels)
    step_rate = decay_rate / total
    gain = residue * jnp.sqrt(jnp.expm1(-2.0 * step_rate) / jnp.expm1(-2.0 * decay_rate))
    h, e = pl.pallas_call(
        functools.partial(tables_kernel, modes, length, total),
        out_shape=(
            jax.ShapeDtypeStruct((length + TILE, channels), f32),
            jax.ShapeDtypeStruct((tiles * modes, channels), f32),
        ),
        compiler_params=params(4),
        name="tables",
    )(decay_rate, gain)

    place = jnp.stack([at // line, at % 2]).astype(jnp.int32)
    near, near_up, near_down, far, far_up, far_down = pieces
    early = pl.pallas_call(
        early_kernel,
        in_specs=[smem] + [vmem] * 5,
        out_specs=vmem,
        out_shape=jax.ShapeDtypeStruct((length, 3 * channels), f32),
        compiler_params=params(12),
        name="early",
    )(place, near, near_up, near_down, far, w_branch)
    first, drive, message = pl.pallas_call(
        functools.partial(project_kernel, modes, length, total),
        in_specs=[smem] + [vmem] * 7,
        out_specs=(vmem,) * 3,
        out_shape=(
            jax.ShapeDtypeStruct((length, channels), f32),
            jax.ShapeDtypeStruct((length, channels), f32),
            jax.ShapeDtypeStruct((seq_count, ROWS, channels), f32),
        ),
        scratch_shapes=[
            pltpu.VMEM((length + TILE, 3 * channels), f32),
            pltpu.VMEM((2, length, channels), f32),
            pltpu.VMEM((ROWS, channels), f32),
        ],
        compiler_params=params(12),
        name="project",
    )(place, early, far_up, far_down, w_branch, taps, decay_rate, e)

    everyone = lax.all_to_all(message, "seq", 0, 0).reshape(seq_count * ROWS, channels)
    skip = skip_gain.reshape(1, channels)
    conv = pl.pallas_call(
        functools.partial(conv_kernel, length),
        in_specs=[vmem] * 3,
        out_specs=vmem,
        out_shape=jax.ShapeDtypeStruct((length, channels), f32),
        scratch_shapes=[
            pltpu.VMEM((length + TILE, channels), f32),
            pltpu.VMEM((TILE, length, channels), f32),
        ],
        compiler_params=params(6),
        name="conv",
    )(drive, h, skip)

    me = lax.axis_index("seq").astype(jnp.int32).reshape(1)
    return pl.pallas_call(
        functools.partial(finish_kernel, modes, length, total, seq_count),
        in_specs=[smem] + [vmem] * 9,
        out_specs=vmem,
        out_shape=jax.ShapeDtypeStruct((length, channels), features.dtype),
        scratch_shapes=[pltpu.VMEM((length, channels), f32)],
        compiler_params=params(6),
        name="finish",
    )(me, everyone, first, conv, taps, decay_rate, gain, skip, h, e)


def solution(mesh):
    placed = (
        P("seq", "shard"),
        P(None, None, "shard"),
        P(),
        P(None, "shard"),
        P(None, "shard"),
        P("shard"),
    )
    return jax.shard_map(
        shards, mesh=mesh, in_specs=placed, out_specs=P("seq", "shard"), check_vma=False
    )
```

```python
import functools

import jax
import jax.numpy as jnp
from jax import lax
from jax.experimental import pallas as pl
from jax.experimental.pallas import tpu as pltpu
from jax.sharding import PartitionSpec as P

TILE = 8
ROWS = 32


def row_tile(ref, row):
    return jnp.broadcast_to(ref[row : row + 1, :], (TILE, ref.shape[1]))


def rise(z):
    value = jnp.full_like(z, 1.0 / 10.0)
    for n in range(9, 1, -1):
        value = (1.0 - z * value) * (1.0 / n)
    return z * (1.0 - z * value)


def prepare_kernel(modes, length, total, rate_ref, residue_ref, w_ref, h_ref, e_ref, gain_ref, held_ref, sem):
    copy = pltpu.make_async_copy(w_ref, held_ref, sem)
    copy.start()
    tiles = length // TILE
    rate = rate_ref[...]
    step = rate * (1.0 / total)
    gain = residue_ref[...] * jnp.sqrt(rise(2.0 * step) / (1.0 - jnp.exp(-2.0 * rate)))
    gain_ref[...] = gain
    lag = jax.lax.broadcasted_iota(jnp.int32, (TILE, step.shape[1]), 0).astype(jnp.float32)
    for q in range(tiles):
        e_ref[q * modes : (q + 1) * modes, :] = jnp.exp(-step * float(TILE * q))
    scaled = [gain[m : m + 1, :] * jnp.exp(-step[m : m + 1, :] * lag) for m in range(modes)]
    h_ref[0:TILE, :] = jnp.zeros((TILE, step.shape[1]), jnp.float32)
    for q in range(tiles):
        total_tile = row_tile(e_ref, q * modes) * scaled[0]
        for m in range(1, modes):
            total_tile = total_tile + row_tile(e_ref, q * modes + m) * scaled[m]
        h_ref[(q + 1) * TILE : (q + 2) * TILE, :] = total_tile
    copy.wait()


def weight_rows(w_ref, owners, block):
    rows = []
    for owner in owners:
        at = pl.ds(pl.multiple_of(owner * block, block), block)
        rows.append(jnp.concatenate([w_ref[b, at, :] for b in range(3)], axis=1))
    return jnp.concatenate(rows, axis=0)


def early_kernel(place_ref, near_ref, near_up_ref, near_down_ref, far_low_ref, far_high_ref, w_ref, acc_ref):
    line, parity = place_ref[0], place_ref[1]
    pairs, _, block = near_ref.shape
    split = near_up_ref.shape[0]
    for k in range(0, pairs, 2):
        lefts, owners = [], []
        for i in (k, k + 1):
            odd = near_up_ref[i] if i < split else near_down_ref[i - split]
            far = far_low_ref[i] if i < split else far_high_ref[i - split]
            lefts += [near_ref[i], odd, far]
            own, other = 2 * pairs * line + 2 * i, 2 * pairs * (1 - line) + 2 * i
            owners += [own + parity, own + 1 - parity, other + parity]
        part = jnp.dot(
            jnp.concatenate(lefts, axis=1),
            weight_rows(w_ref, owners, block),
            preferred_element_type=jnp.float32,
        )
        acc_ref[...] = part if k == 0 else acc_ref[...] + part


def project_kernel(
    modes, length, total, place_ref, early_ref, far_up_ref, far_down_ref, w_ref, taps_ref, rate_ref,
    e_ref, first_ref, drive_ref, message_ref, proj_ref, filt_ref, state_ref,
):
    line, parity = place_ref[0], place_ref[1]
    split, _, block = far_up_ref.shape
    pairs = 2 * split
    channels = drive_ref.shape[1]
    acc = early_ref[...]
    for ref, start in ((far_up_ref, 0), (far_down_ref, split)):
        owners = [2 * pairs * (1 - line) + 2 * (start + k) + 1 - parity for k in range(split)]
        left = jnp.concatenate([ref[k] for k in range(split)], axis=1)
        acc = acc + jnp.dot(
            left, weight_rows(w_ref, owners, block), preferred_element_type=jnp.float32
        )

    pad = TILE
    proj_ref[0:pad, :] = jnp.zeros((pad, 3 * channels), jnp.float32)
    proj_ref[pad:, :] = acc.astype(jnp.bfloat16).astype(jnp.float32)
    for b in range(3):
        cols = slice(b * channels, (b + 1) * channels)
        value = taps_ref[b : b + 1, :] * proj_ref[pad : pad + length, cols]
        value = value + taps_ref[3 + b : 4 + b, :] * proj_ref[pad - 1 : pad - 1 + length, cols]
        value = value + taps_ref[6 + b : 7 + b, :] * proj_ref[pad - 2 : pad - 2 + length, cols]
        if b == 0:
            first_ref[...] = value
        else:
            filt_ref[b - 1] = value
    drive_ref[...] = filt_ref[0] * filt_ref[1]
    row = jax.lax.broadcasted_iota(jnp.int32, (TILE, channels), 0)
    drive_ref[0:TILE, :] = jnp.where(row < 2, 0.0, drive_ref[0:TILE, :])
    lag = (TILE - 1 - row).astype(jnp.float32)
    tiles = length // TILE
    pieces = [drive_ref[q * TILE : (q + 1) * TILE, :] for q in range(tiles)]
    step = rate_ref[...] * (1.0 / total)
    for m in range(modes):
        state = row_tile(e_ref, (tiles - 1) * modes + m) * pieces[0]
        for q in range(1, tiles):
            state = state + row_tile(e_ref, (tiles - 1 - q) * modes + m) * pieces[q]
        state = state * jnp.exp(-step[m : m + 1, :] * lag)
        state_ref[m : m + 1, :] = jnp.sum(state, axis=0, keepdims=True)
    one, two, three = channels, 2 * channels, 3 * channels
    head, tail = pad, pad + length - 2
    spots = [
        (head, one, two), (head, two, three), (head + 1, one, two), (head + 1, two, three),
        (tail, one, two), (tail, two, three), (tail + 1, one, two), (tail + 1, two, three),
        (tail, 0, one), (tail + 1, 0, one),
    ]
    for k, (r, lo, hi) in enumerate(spots):
        state_ref[modes + k : modes + k + 1, :] = proj_ref[r : r + 1, lo:hi]
    used = modes + len(spots)
    state_ref[used:ROWS, :] = jnp.zeros((ROWS - used, channels), jnp.float32)
    for s in range(message_ref.shape[0]):
        message_ref[s] = state_ref[...]


def conv_kernel(length, drive_ref, h_ref, skip_ref, conv_ref, pad_ref, lag_ref):
    channels = drive_ref.shape[1]
    tiles = length // TILE
    pad_ref[0:TILE, :] = jnp.zeros((TILE, channels), jnp.float32)
    pad_ref[TILE:, :] = drive_ref[...]
    for j in range(TILE):
        lag_ref[j] = pad_ref[TILE - j : TILE - j + length, :]

    group = 8
    for g in range(tiles // group):
        low = g * group

        def over_lags(j, accs):
            accs = list(accs)
            window = [lag_ref[j, pl.ds((low + i) * TILE, TILE), :] for i in range(group)]
            for p in range(low + group):
                weight = jnp.broadcast_to(h_ref[pl.ds(TILE * (p + 1) + j, 1), :], (TILE, channels))
                for i in range(group):
                    if low + i - p >= 0:
                        accs[i] = accs[i] + weight * window[i]
                below = low - p - 1
                fresh = lag_ref[j, pl.ds(below * TILE, TILE), :] if below >= 0 else None
                window = [fresh] + window[:-1]
            return tuple(accs)

        accs = tuple(skip_ref[...] * drive_ref[(low + i) * TILE : (low + i + 1) * TILE, :] for i in range(group))
        accs = lax.fori_loop(0, TILE, over_lags, accs)
        for i in range(group):
            conv_ref[(low + i) * TILE : (low + i + 1) * TILE, :] = accs[i]


def finish_kernel(
    modes, length, total, seq_count, me_ref, all_ref, first_ref, conv_ref, taps_ref, rate_ref,
    gain_ref, skip_ref, h_ref, e_ref, out_ref, value_ref,
):
    me = me_ref[0]
    channels = conv_ref.shape[1]
    tiles = length // TILE
    step = rate_ref[...] * (1.0 / total)

    def tap(j, b):
        return taps_ref[3 * j + b : 3 * j + b + 1, :]

    def rows(k):
        return all_ref[pl.ds(modes + k, seq_count, stride=ROWS), :]

    order = jax.lax.broadcasted_iota(jnp.int32, (seq_count, channels), 0)

    def before(k):
        return jnp.where(order == 0, 0.0, pltpu.roll(rows(k), 1, 0))

    starts = [None, None]
    for b in (1, 2):
        head0, head1 = rows(b - 1), rows(2 + b - 1)
        rim0, rim1 = before(4 + b - 1), before(6 + b - 1)
        row0 = tap(0, b) * head0 + tap(1, b) * rim1 + tap(2, b) * rim0
        row1 = tap(0, b) * head1 + tap(1, b) * head0 + tap(2, b) * rim1
        starts = [row0, row1] if b == 1 else [starts[0] * row0, starts[1] * row1]
    start0, start1 = starts
    late0 = jnp.exp(-step * float(length - 1))
    late1 = jnp.exp(-step * float(length - 2))
    fade = jnp.exp(-step * float(length))
    incoming = jnp.zeros((modes, channels), jnp.float32)
    for j in range(seq_count):
        state = all_ref[j * ROWS : j * ROWS + modes, :]
        state = state + late0 * start0[j : j + 1, :] + late1 * start1[j : j + 1, :]
        incoming = jnp.where(j < me, incoming * fade + state, incoming)

    row = jax.lax.broadcasted_iota(jnp.int32, (TILE, channels), 0)
    mine0 = jnp.sum(jnp.where(order == me, start0, 0.0), axis=0, keepdims=True)
    mine1 = jnp.sum(jnp.where(order == me, start1, 0.0), axis=0, keepdims=True)
    rim0 = jnp.sum(jnp.where(order == me - 1, rows(8), 0.0), axis=0, keepdims=True)
    rim1 = jnp.sum(jnp.where(order == me - 1, rows(9), 0.0), axis=0, keepdims=True)
    extra0 = tap(1, 0) * rim1 + tap(2, 0) * rim0
    extra1 = tap(2, 0) * rim1

    lead = (row + 1).astype(jnp.float32)
    heads = []
    for m in range(modes):
        scale = gain_ref[m : m + 1, :] * incoming[m : m + 1, :]
        heads.append(scale * jnp.exp(-step[m : m + 1, :] * lead))
    skip = skip_ref[...]
    for q in range(tiles):
        at = slice(q * TILE, (q + 1) * TILE)
        value = conv_ref[at, :]
        value = value + mine0 * h_ref[(q + 1) * TILE : (q + 2) * TILE, :]
        value = value + mine1 * h_ref[(q + 1) * TILE - 1 : (q + 2) * TILE - 1, :]
        for m in range(modes):
            value = value + row_tile(e_ref, q * modes + m) * heads[m]
        gate = first_ref[at, :]
        if q == 0:
            value = value + jnp.where(row == 0, skip * mine0, jnp.where(row == 1, skip * mine1, 0.0))
            gate = gate + jnp.where(row == 0, extra0, jnp.where(row == 1, extra1, 0.0))
        value_ref[at, :] = gate * value
    out_ref[...] = value_ref[...].astype(out_ref.dtype)


def gather_features(features):
    shard_count = lax.axis_size("shard")
    line = shard_count // 2
    pairs = line // 2
    groups = [[l * line + 2 * q + p for q in range(pairs)] for l in range(2) for p in range(2)]
    across = [(i, (i + line) % shard_count) for i in range(shard_count)]
    up = [(l * line + z, l * line + (z - 1) % line) for l in range(2) for z in range(line)]
    down = [(l * line + z, l * line + (z + 1) % line) for l in range(2) for z in range(line)]
    half = pairs // 2

    near = lax.all_gather(features, "shard", axis=0, axis_index_groups=groups)
    low, high = near[:half], near[half:]
    far_low = lax.ppermute(low, "shard", across)
    far_high = lax.ppermute(high, "shard", across)
    near_up = lax.ppermute(low, "shard", up)
    near_down = lax.ppermute(high, "shard", down)
    far_up = lax.ppermute(far_low, "shard", up)
    far_down = lax.ppermute(far_high, "shard", down)
    return near, near_up, near_down, far_low, far_high, far_up, far_down


def shards(features, in_proj, short_filter, residue, decay_rate, skip_gain):
    length = features.shape[0]
    channels = in_proj.shape[2]
    modes = residue.shape[0]
    seq_count = lax.axis_size("seq")
    line = lax.axis_size("shard") // 2
    total = length * seq_count
    tiles = length // TILE
    f32 = jnp.float32
    vmem = pl.BlockSpec(memory_space=pltpu.VMEM)
    smem = pl.BlockSpec(memory_space=pltpu.SMEM)

    def params(mebibytes):
        return pltpu.CompilerParams(vmem_limit_bytes=mebibytes << 20)

    pieces = gather_features(features)
    w_branch = in_proj.transpose(1, 0, 2)
    at = lax.axis_index("shard")
    taps = lax.dynamic_slice_in_dim(short_filter, at * channels, channels, 2).reshape(-1, channels)
    hbm = pl.BlockSpec(memory_space=pltpu.HBM)
    h, e, gain, w_held = pl.pallas_call(
        functools.partial(prepare_kernel, modes, length, total),
        in_specs=[vmem, vmem, hbm],
        out_specs=(vmem,) * 4,
        out_shape=(
            jax.ShapeDtypeStruct((length + TILE, channels), f32),
            jax.ShapeDtypeStruct((tiles * modes, channels), f32),
            jax.ShapeDtypeStruct((modes, channels), f32),
            jax.ShapeDtypeStruct(w_branch.shape, w_branch.dtype),
        ),
        scratch_shapes=[pltpu.SemaphoreType.DMA],
        compiler_params=params(8),
        name="prepare",
    )(decay_rate, residue, w_branch)

    place = jnp.stack([at // line, at % 2]).astype(jnp.int32)
    near, near_up, near_down, far_low, far_high, far_up, far_down = pieces
    early = pl.pallas_call(
        early_kernel,
        in_specs=[smem] + [vmem] * 6,
        out_specs=vmem,
        out_shape=jax.ShapeDtypeStruct((length, 3 * channels), f32),
        compiler_params=params(12),
        name="early",
    )(place, near, near_up, near_down, far_low, far_high, w_held)
    first, drive, message = pl.pallas_call(
        functools.partial(project_kernel, modes, length, total),
        in_specs=[smem] + [vmem] * 7,
        out_specs=(vmem,) * 3,
        out_shape=(
            jax.ShapeDtypeStruct((length, channels), f32),
            jax.ShapeDtypeStruct((length, channels), f32),
            jax.ShapeDtypeStruct((seq_count, ROWS, channels), f32),
        ),
        scratch_shapes=[
            pltpu.VMEM((length + TILE, 3 * channels), f32),
            pltpu.VMEM((2, length, channels), f32),
            pltpu.VMEM((ROWS, channels), f32),
        ],
        compiler_params=params(12),
        name="project",
    )(place, early, far_up, far_down, w_held, taps, decay_rate, e)

    everyone = lax.all_to_all(message, "seq", 0, 0).reshape(seq_count * ROWS, channels)
    skip = skip_gain.reshape(1, channels)
    conv = pl.pallas_call(
        functools.partial(conv_kernel, length),
        in_specs=[vmem] * 3,
        out_specs=vmem,
        out_shape=jax.ShapeDtypeStruct((length, channels), f32),
        scratch_shapes=[
            pltpu.VMEM((length + TILE, channels), f32),
            pltpu.VMEM((TILE, length, channels), f32),
        ],
        compiler_params=params(6),
        name="conv",
    )(drive, h, skip)

    me = lax.axis_index("seq").astype(jnp.int32).reshape(1)
    return pl.pallas_call(
        functools.partial(finish_kernel, modes, length, total, seq_count),
        in_specs=[smem] + [vmem] * 9,
        out_specs=vmem,
        out_shape=jax.ShapeDtypeStruct((length, channels), features.dtype),
        scratch_shapes=[pltpu.VMEM((length, channels), f32)],
        compiler_params=params(6),
        name="finish",
    )(me, everyone, first, conv, taps, decay_rate, gain, skip, h, e)


def solution(mesh):
    placed = (
        P("seq", "shard"),
        P(None, None, "shard"),
        P(),
        P(None, "shard"),
        P(None, "shard"),
        P("shard"),
    )
    return jax.shard_map(
        shards, mesh=mesh, in_specs=placed, out_specs=P("seq", "shard"), check_vma=False
    )
```

```python
import functools

import jax
import jax.numpy as jnp
from jax import lax
from jax.experimental import pallas as pl
from jax.experimental.pallas import tpu as pltpu
from jax.sharding import PartitionSpec as P

TILE = 8
ROWS = 32


def row_tile(ref, row):
    return jnp.broadcast_to(ref[row : row + 1, :], (TILE, ref.shape[1]))


def rise(z):
    value = jnp.full_like(z, 1.0 / 10.0)
    for n in range(9, 1, -1):
        value = (1.0 - z * value) * (1.0 / n)
    return z * (1.0 - z * value)


def tables_kernel(modes, length, total, rate_ref, residue_ref, h_ref, e_ref, gain_ref):
    tiles = length // TILE
    rate = rate_ref[...]
    step = rate * (1.0 / total)
    gain_ref[...] = residue_ref[...] * jnp.sqrt(rise(2.0 * step) / (1.0 - jnp.exp(-2.0 * rate)))
    lane = jax.lax.broadcasted_iota(jnp.int32, (TILE, step.shape[1]), 0).astype(jnp.float32)
    for q in range(tiles):
        e_ref[q * modes : (q + 1) * modes, :] = jnp.exp(-step * float(TILE * q))
    scaled = [gain_ref[m : m + 1, :] * jnp.exp(-step[m : m + 1, :] * lane) for m in range(modes)]
    h_ref[0:TILE, :] = jnp.zeros((TILE, step.shape[1]), jnp.float32)
    for q in range(tiles):
        total_tile = row_tile(e_ref, q * modes) * scaled[0]
        for m in range(1, modes):
            total_tile = total_tile + row_tile(e_ref, q * modes + m) * scaled[m]
        h_ref[(q + 1) * TILE : (q + 2) * TILE, :] = total_tile


def weight_rows(w_ref, owners, block):
    rows = []
    for owner in owners:
        at = pl.ds(pl.multiple_of(owner * block, block), block)
        rows.append(jnp.concatenate([w_ref[b, at, :] for b in range(3)], axis=1))
    return jnp.concatenate(rows, axis=0)


def early_kernel(place_ref, near_ref, near_up_ref, near_down_ref, far_ref, w_ref, acc_ref):
    line, parity = place_ref[0], place_ref[1]
    pairs, _, block = near_ref.shape
    split = near_up_ref.shape[0]
    for k in range(0, pairs, 2):
        lefts, owners = [], []
        for i in (k, k + 1):
            odd = near_up_ref[i] if i < split else near_down_ref[i - split]
            lefts += [near_ref[i], odd, far_ref[i]]
            own, other = 2 * pairs * line + 2 * i, 2 * pairs * (1 - line) + 2 * i
            owners += [own + parity, own + 1 - parity, other + parity]
        part = jnp.dot(
            jnp.concatenate(lefts, axis=1),
            weight_rows(w_ref, owners, block),
            preferred_element_type=jnp.float32,
        )
        acc_ref[...] = part if k == 0 else acc_ref[...] + part


def project_kernel(
    modes, length, total, place_ref, early_ref, far_up_ref, far_down_ref, w_ref, taps_ref, rate_ref,
    e_ref, lead_ref, drive_ref, message_ref, pair_ref, state_ref,
):
    line, parity = place_ref[0], place_ref[1]
    split, _, block = far_up_ref.shape
    pairs = split + far_down_ref.shape[0]
    channels = drive_ref.shape[1]
    owners = [2 * pairs * (1 - line) + 2 * k + 1 - parity for k in range(pairs)]
    left = [far_up_ref[k] if k < split else far_down_ref[k - split] for k in range(pairs)]
    acc = early_ref[...] + jnp.dot(
        jnp.concatenate(left, axis=1),
        weight_rows(w_ref, owners, block),
        preferred_element_type=jnp.float32,
    )
    proj = acc.astype(jnp.bfloat16).astype(jnp.float32)
    pad = TILE
    one, two, three = channels, 2 * channels, 3 * channels
    lead_ref[0:pad, :] = jnp.zeros((pad, channels), jnp.float32)
    lead_ref[pad:, :] = proj[:, 0:one]
    pair_ref[0:pad, :] = jnp.zeros((pad, two), jnp.float32)
    pair_ref[pad:, :] = proj[:, one:three]

    row = jax.lax.broadcasted_iota(jnp.int32, (TILE, channels), 0)
    taps = [[row_tile(taps_ref, 3 * j + b) for j in range(3)] for b in (1, 2)]
    tiles = length // TILE
    states = [None] * modes
    for q in range(tiles):
        drive = None
        for b in range(2):
            cols = slice(b * channels, (b + 1) * channels)
            at = pad + q * TILE
            value = taps[b][0] * pair_ref[at : at + TILE, cols]
            value = value + taps[b][1] * pair_ref[at - 1 : at - 1 + TILE, cols]
            value = value + taps[b][2] * pair_ref[at - 2 : at - 2 + TILE, cols]
            drive = value if b == 0 else drive * value
        if q == 0:
            drive = jnp.where(row < 2, 0.0, drive)
        drive_ref[q * TILE : (q + 1) * TILE, :] = drive
        for m in range(modes):
            term = row_tile(e_ref, (tiles - 1 - q) * modes + m) * drive
            states[m] = term if q == 0 else states[m] + term
    step = rate_ref[...] * (1.0 / total)
    lag = (TILE - 1 - row).astype(jnp.float32)
    for m in range(modes):
        state = states[m] * jnp.exp(-step[m : m + 1, :] * lag)
        state_ref[m : m + 1, :] = jnp.sum(state, axis=0, keepdims=True)
    head, tail = pad, pad + length - 2
    spots = [(r, b) for r in (head, head + 1, tail, tail + 1) for b in (0, 1)]
    for k, (r, b) in enumerate(spots):
        state_ref[modes + k : modes + k + 1, :] = pair_ref[r : r + 1, b * channels : (b + 1) * channels]
    used = modes + len(spots)
    state_ref[used : used + 2, :] = lead_ref[tail : tail + 2, :]
    state_ref[used + 2 : ROWS, :] = jnp.zeros((ROWS - used - 2, channels), jnp.float32)
    message = state_ref[...]
    for s in range(message_ref.shape[0]):
        message_ref[s] = message


def conv_kernel(length, drive_ref, h_ref, skip_ref, lead_ref, taps_ref, conv_ref, first_ref, pad_ref, lag_ref):
    channels = drive_ref.shape[1]
    tiles = length // TILE
    pad_ref[0:TILE, :] = jnp.zeros((TILE, channels), jnp.float32)
    pad_ref[TILE:, :] = drive_ref[...]
    for j in range(TILE):
        lag_ref[j] = pad_ref[TILE - j : TILE - j + length, :]

    for q in range(tiles):
        at = (q + 1) * TILE
        value = row_tile(taps_ref, 0) * lead_ref[at : at + TILE, :]
        value = value + row_tile(taps_ref, 3) * lead_ref[at - 1 : at - 1 + TILE, :]
        value = value + row_tile(taps_ref, 6) * lead_ref[at - 2 : at - 2 + TILE, :]
        first_ref[q * TILE : (q + 1) * TILE, :] = value

    group = 8
    for g in range(tiles // group):
        low = g * group

        def over_lags(j, accs):
            accs = list(accs)
            window = [lag_ref[j, pl.ds((low + i) * TILE, TILE), :] for i in range(group)]
            for p in range(low + group):
                weight = jnp.broadcast_to(h_ref[pl.ds(TILE * (p + 1) + j, 1), :], (TILE, channels))
                for i in range(group):
                    if low + i - p >= 0:
                        accs[i] = accs[i] + weight * window[i]
                below = low - p - 1
                fresh = lag_ref[j, pl.ds(below * TILE, TILE), :] if below >= 0 else None
                window = [fresh] + window[:-1]
            return tuple(accs)

        accs = tuple(skip_ref[...] * drive_ref[(low + i) * TILE : (low + i + 1) * TILE, :] for i in range(group))
        accs = lax.fori_loop(0, TILE, over_lags, accs)
        for i in range(group):
            conv_ref[(low + i) * TILE : (low + i + 1) * TILE, :] = accs[i]


def finish_kernel(
    modes, length, total, seq_count, me_ref, all_ref, first_ref, conv_ref, taps_ref, rate_ref,
    gain_ref, skip_ref, h_ref, e_ref, out_ref, value_ref,
):
    me = me_ref[0]
    channels = conv_ref.shape[1]
    tiles = length // TILE
    step = rate_ref[...] * (1.0 / total)

    def tap(j, b):
        return taps_ref[3 * j + b : 3 * j + b + 1, :]

    def rows(k):
        return all_ref[pl.ds(modes + k, seq_count, stride=ROWS), :]

    order = jax.lax.broadcasted_iota(jnp.int32, (seq_count, channels), 0)

    def before(k):
        return jnp.where(order == 0, 0.0, pltpu.roll(rows(k), 1, 0))

    starts = [None, None]
    for b in (1, 2):
        head0, head1 = rows(b - 1), rows(2 + b - 1)
        rim0, rim1 = before(4 + b - 1), before(6 + b - 1)
        row0 = tap(0, b) * head0 + tap(1, b) * rim1 + tap(2, b) * rim0
        row1 = tap(0, b) * head1 + tap(1, b) * head0 + tap(2, b) * rim1
        starts = [row0, row1] if b == 1 else [starts[0] * row0, starts[1] * row1]
    start0, start1 = starts
    late0 = jnp.exp(-step * float(length - 1))
    late1 = jnp.exp(-step * float(length - 2))
    fade = jnp.exp(-step * float(length))
    incoming = jnp.zeros((modes, channels), jnp.float32)
    for j in range(seq_count):
        state = all_ref[j * ROWS : j * ROWS + modes, :]
        state = state + late0 * start0[j : j + 1, :] + late1 * start1[j : j + 1, :]
        incoming = jnp.where(j < me, incoming * fade + state, incoming)

    row = jax.lax.broadcasted_iota(jnp.int32, (TILE, channels), 0)
    mine0 = jnp.sum(jnp.where(order == me, start0, 0.0), axis=0, keepdims=True)
    mine1 = jnp.sum(jnp.where(order == me, start1, 0.0), axis=0, keepdims=True)
    rim0 = jnp.sum(jnp.where(order == me - 1, rows(8), 0.0), axis=0, keepdims=True)
    rim1 = jnp.sum(jnp.where(order == me - 1, rows(9), 0.0), axis=0, keepdims=True)
    extra0 = tap(1, 0) * rim1 + tap(2, 0) * rim0
    extra1 = tap(2, 0) * rim1

    lead = (row + 1).astype(jnp.float32)
    heads = []
    for m in range(modes):
        scale = gain_ref[m : m + 1, :] * incoming[m : m + 1, :]
        heads.append(scale * jnp.exp(-step[m : m + 1, :] * lead))
    skip = skip_ref[...]
    for q in range(tiles):
        at = slice(q * TILE, (q + 1) * TILE)
        value = conv_ref[at, :]
        value = value + mine0 * h_ref[(q + 1) * TILE : (q + 2) * TILE, :]
        value = value + mine1 * h_ref[(q + 1) * TILE - 1 : (q + 2) * TILE - 1, :]
        for m in range(modes):
            value = value + row_tile(e_ref, q * modes + m) * heads[m]
        gate = first_ref[at, :]
        if q == 0:
            value = value + jnp.where(row == 0, skip * mine0, jnp.where(row == 1, skip * mine1, 0.0))
            gate = gate + jnp.where(row == 0, extra0, jnp.where(row == 1, extra1, 0.0))
        value_ref[at, :] = gate * value
    out_ref[...] = value_ref[...].astype(out_ref.dtype)


def gather_features(features):
    shard_count = lax.axis_size("shard")
    line = shard_count // 2
    pairs = line // 2
    groups = [[l * line + 2 * q + p for q in range(pairs)] for l in range(2) for p in range(2)]
    across = [(i, (i + line) % shard_count) for i in range(shard_count)]
    up = [(l * line + z, l * line + (z - 1) % line) for l in range(2) for z in range(line)]
    down = [(l * line + z, l * line + (z + 1) % line) for l in range(2) for z in range(line)]
    half = pairs // 2

    near = lax.all_gather(features, "shard", axis=0, axis_index_groups=groups)
    far = lax.ppermute(near, "shard", across)
    near_up = lax.ppermute(near[:half], "shard", up)
    near_down = lax.ppermute(near[half:], "shard", down)
    most = half + 1
    far_up = lax.ppermute(far[:most], "shard", up)
    far_down = lax.ppermute(far[most:], "shard", down)
    return near, near_up, near_down, far, far_up, far_down


def shards(features, in_proj, short_filter, residue, decay_rate, skip_gain):
    length = features.shape[0]
    channels = in_proj.shape[2]
    modes = residue.shape[0]
    seq_count = lax.axis_size("seq")
    line = lax.axis_size("shard") // 2
    total = length * seq_count
    tiles = length // TILE
    f32 = jnp.float32
    vmem = pl.BlockSpec(memory_space=pltpu.VMEM)
    smem = pl.BlockSpec(memory_space=pltpu.SMEM)

    def params(mebibytes):
        return pltpu.CompilerParams(vmem_limit_bytes=mebibytes << 20)

    pieces = gather_features(features)
    w_branch = in_proj.transpose(1, 0, 2)
    at = lax.axis_index("shard")
    taps = lax.dynamic_slice_in_dim(short_filter, at * channels, channels, 2).reshape(-1, channels)
    h, e, gain = pl.pallas_call(
        functools.partial(tables_kernel, modes, length, total),
        out_shape=(
            jax.ShapeDtypeStruct((length + TILE, channels), f32),
            jax.ShapeDtypeStruct((tiles * modes, channels), f32),
            jax.ShapeDtypeStruct((modes, channels), f32),
        ),
        compiler_params=params(4),
        name="tables",
    )(decay_rate, residue)

    place = jnp.stack([at // line, at % 2]).astype(jnp.int32)
    near, near_up, near_down, far, far_up, far_down = pieces
    early = pl.pallas_call(
        early_kernel,
        in_specs=[smem] + [vmem] * 5,
        out_specs=vmem,
        out_shape=jax.ShapeDtypeStruct((length, 3 * channels), f32),
        compiler_params=params(12),
        name="early",
    )(place, near, near_up, near_down, far, w_branch)
    lead, drive, message = pl.pallas_call(
        functools.partial(project_kernel, modes, length, total),
        in_specs=[smem] + [vmem] * 7,
        out_specs=(vmem,) * 3,
        out_shape=(
            jax.ShapeDtypeStruct((length + TILE, channels), f32),
            jax.ShapeDtypeStruct((length, channels), f32),
            jax.ShapeDtypeStruct((seq_count, ROWS, channels), f32),
        ),
        scratch_shapes=[
            pltpu.VMEM((length + TILE, 2 * channels), f32),
            pltpu.VMEM((ROWS, channels), f32),
        ],
        compiler_params=params(12),
        name="project",
    )(place, early, far_up, far_down, w_branch, taps, decay_rate, e)

    everyone = lax.all_to_all(message, "seq", 0, 0).reshape(seq_count * ROWS, channels)
    skip = skip_gain.reshape(1, channels)
    conv, first = pl.pallas_call(
        functools.partial(conv_kernel, length),
        in_specs=[vmem] * 5,
        out_specs=(vmem,) * 2,
        out_shape=(jax.ShapeDtypeStruct((length, channels), f32),) * 2,
        scratch_shapes=[
            pltpu.VMEM((length + TILE, channels), f32),
            pltpu.VMEM((TILE, length, channels), f32),
        ],
        compiler_params=params(6),
        name="conv",
    )(drive, h, skip, lead, taps)

    me = lax.axis_index("seq").astype(jnp.int32).reshape(1)
    return pl.pallas_call(
        functools.partial(finish_kernel, modes, length, total, seq_count),
        in_specs=[smem] + [vmem] * 9,
        out_specs=vmem,
        out_shape=jax.ShapeDtypeStruct((length, channels), features.dtype),
        scratch_shapes=[pltpu.VMEM((length, channels), f32)],
        compiler_params=params(6),
        name="finish",
    )(me, everyone, first, conv, taps, decay_rate, gain, skip, h, e)


def solution(mesh):
    placed = (
        P("seq", "shard"),
        P(None, None, "shard"),
        P(),
        P(None, "shard"),
        P(None, "shard"),
        P("shard"),
    )
    return jax.shard_map(
        shards, mesh=mesh, in_specs=placed, out_specs=P("seq", "shard"), check_vma=False
    )
```

```python
import functools

import jax
import jax.numpy as jnp
from jax import lax
from jax.experimental import pallas as pl
from jax.experimental.pallas import tpu as pltpu
from jax.sharding import PartitionSpec as P

TILE = 8
ROWS = 32


def row_tile(ref, row):
    return jnp.broadcast_to(ref[row : row + 1, :], (TILE, ref.shape[1]))


def rise(z):
    value = jnp.full_like(z, 1.0 / 10.0)
    for n in range(9, 1, -1):
        value = (1.0 - z * value) * (1.0 / n)
    return z * (1.0 - z * value)


def tables_kernel(modes, length, total, rate_ref, residue_ref, h_ref, e_ref, gain_ref):
    tiles = length // TILE
    rate = rate_ref[...]
    step = rate * (1.0 / total)
    gain_ref[...] = residue_ref[...] * jnp.sqrt(rise(2.0 * step) / (1.0 - jnp.exp(-2.0 * rate)))
    lane = jax.lax.broadcasted_iota(jnp.int32, (TILE, step.shape[1]), 0).astype(jnp.float32)
    for q in range(tiles):
        e_ref[q * modes : (q + 1) * modes, :] = jnp.exp(-step * float(TILE * q))
    scaled = [gain_ref[m : m + 1, :] * jnp.exp(-step[m : m + 1, :] * lane) for m in range(modes)]
    h_ref[0:TILE, :] = jnp.zeros((TILE, step.shape[1]), jnp.float32)
    for q in range(tiles):
        total_tile = row_tile(e_ref, q * modes) * scaled[0]
        for m in range(1, modes):
            total_tile = total_tile + row_tile(e_ref, q * modes + m) * scaled[m]
        h_ref[(q + 1) * TILE : (q + 2) * TILE, :] = total_tile


def weight_rows(w_ref, owners, block):
    rows = []
    for owner in owners:
        at = pl.ds(pl.multiple_of(owner * block, block), block)
        rows.append(jnp.concatenate([w_ref[b, at, :] for b in range(3)], axis=1))
    return jnp.concatenate(rows, axis=0)


def early_kernel(place_ref, near_ref, odd_ref, far_ref, w_ref, acc_ref):
    line, parity = place_ref[0], place_ref[1]
    pairs, _, block = near_ref.shape
    for k in range(0, pairs, 2):
        lefts, owners = [], []
        for i in (k, k + 1):
            lefts += [near_ref[i], odd_ref[i], far_ref[i]]
            own, other = 2 * pairs * line + 2 * i, 2 * pairs * (1 - line) + 2 * i
            owners += [own + parity, own + 1 - parity, other + parity]
        part = jnp.dot(
            jnp.concatenate(lefts, axis=1),
            weight_rows(w_ref, owners, block),
            preferred_element_type=jnp.float32,
        )
        acc_ref[...] = part if k == 0 else acc_ref[...] + part


def project_kernel(
    modes, length, total, place_ref, early_ref, far_up_ref, far_down_ref, w_ref, taps_ref, rate_ref,
    e_ref, lead_ref, drive_ref, message_ref, pair_ref, state_ref,
):
    line, parity = place_ref[0], place_ref[1]
    split, _, block = far_up_ref.shape
    pairs = split + far_down_ref.shape[0]
    channels = drive_ref.shape[1]
    owners = [2 * pairs * (1 - line) + 2 * k + 1 - parity for k in range(pairs)]
    left = [far_up_ref[k] if k < split else far_down_ref[k - split] for k in range(pairs)]
    acc = early_ref[...] + jnp.dot(
        jnp.concatenate(left, axis=1),
        weight_rows(w_ref, owners, block),
        preferred_element_type=jnp.float32,
    )
    proj = acc.astype(jnp.bfloat16).astype(jnp.float32)
    pad = TILE
    one, two, three = channels, 2 * channels, 3 * channels
    lead_ref[0:pad, :] = jnp.zeros((pad, channels), jnp.float32)
    lead_ref[pad:, :] = proj[:, 0:one]
    pair_ref[0:pad, :] = jnp.zeros((pad, two), jnp.float32)
    pair_ref[pad:, :] = proj[:, one:three]

    row = jax.lax.broadcasted_iota(jnp.int32, (TILE, channels), 0)
    taps = [[row_tile(taps_ref, 3 * j + b) for j in range(3)] for b in (1, 2)]
    tiles = length // TILE
    states = [None] * modes
    for q in range(tiles):
        drive = None
        for b in range(2):
            cols = slice(b * channels, (b + 1) * channels)
            at = pad + q * TILE
            value = taps[b][0] * pair_ref[at : at + TILE, cols]
            value = value + taps[b][1] * pair_ref[at - 1 : at - 1 + TILE, cols]
            value = value + taps[b][2] * pair_ref[at - 2 : at - 2 + TILE, cols]
            drive = value if b == 0 else drive * value
        if q == 0:
            drive = jnp.where(row < 2, 0.0, drive)
        drive_ref[q * TILE : (q + 1) * TILE, :] = drive
        for m in range(modes):
            term = row_tile(e_ref, (tiles - 1 - q) * modes + m) * drive
            states[m] = term if q == 0 else states[m] + term
    step = rate_ref[...] * (1.0 / total)
    lag = (TILE - 1 - row).astype(jnp.float32)
    for m in range(modes):
        state = states[m] * jnp.exp(-step[m : m + 1, :] * lag)
        state_ref[m : m + 1, :] = jnp.sum(state, axis=0, keepdims=True)
    head, tail = pad, pad + length - 2
    spots = [(r, b) for r in (head, head + 1, tail, tail + 1) for b in (0, 1)]
    for k, (r, b) in enumerate(spots):
        state_ref[modes + k : modes + k + 1, :] = pair_ref[r : r + 1, b * channels : (b + 1) * channels]
    used = modes + len(spots)
    state_ref[used : used + 2, :] = lead_ref[tail : tail + 2, :]
    state_ref[used + 2 : ROWS, :] = jnp.zeros((ROWS - used - 2, channels), jnp.float32)
    message = state_ref[...]
    for s in range(message_ref.shape[0]):
        message_ref[s] = message


def conv_kernel(length, drive_ref, h_ref, skip_ref, lead_ref, taps_ref, conv_ref, first_ref, pad_ref, lag_ref):
    channels = drive_ref.shape[1]
    tiles = length // TILE
    pad_ref[0:TILE, :] = jnp.zeros((TILE, channels), jnp.float32)
    pad_ref[TILE:, :] = drive_ref[...]
    for j in range(TILE):
        lag_ref[j] = pad_ref[TILE - j : TILE - j + length, :]

    for q in range(tiles):
        at = (q + 1) * TILE
        value = row_tile(taps_ref, 0) * lead_ref[at : at + TILE, :]
        value = value + row_tile(taps_ref, 3) * lead_ref[at - 1 : at - 1 + TILE, :]
        value = value + row_tile(taps_ref, 6) * lead_ref[at - 2 : at - 2 + TILE, :]
        first_ref[q * TILE : (q + 1) * TILE, :] = value

    group = 8
    for g in range(tiles // group):
        low = g * group

        def over_lags(j, accs):
            accs = list(accs)
            window = [lag_ref[j, pl.ds((low + i) * TILE, TILE), :] for i in range(group)]
            for p in range(low + group):
                weight = jnp.broadcast_to(h_ref[pl.ds(TILE * (p + 1) + j, 1), :], (TILE, channels))
                for i in range(group):
                    if low + i - p >= 0:
                        accs[i] = accs[i] + weight * window[i]
                below = low - p - 1
                fresh = lag_ref[j, pl.ds(below * TILE, TILE), :] if below >= 0 else None
                window = [fresh] + window[:-1]
            return tuple(accs)

        accs = tuple(skip_ref[...] * drive_ref[(low + i) * TILE : (low + i + 1) * TILE, :] for i in range(group))
        accs = lax.fori_loop(0, TILE, over_lags, accs)
        for i in range(group):
            conv_ref[(low + i) * TILE : (low + i + 1) * TILE, :] = accs[i]


def finish_kernel(
    modes, length, total, seq_count, me_ref, all_ref, first_ref, conv_ref, taps_ref, rate_ref,
    gain_ref, skip_ref, h_ref, e_ref, out_ref, value_ref,
):
    me = me_ref[0]
    channels = conv_ref.shape[1]
    tiles = length // TILE
    step = rate_ref[...] * (1.0 / total)

    def tap(j, b):
        return taps_ref[3 * j + b : 3 * j + b + 1, :]

    def rows(k):
        return all_ref[pl.ds(modes + k, seq_count, stride=ROWS), :]

    order = jax.lax.broadcasted_iota(jnp.int32, (seq_count, channels), 0)

    def before(k):
        return jnp.where(order == 0, 0.0, pltpu.roll(rows(k), 1, 0))

    starts = [None, None]
    for b in (1, 2):
        head0, head1 = rows(b - 1), rows(2 + b - 1)
        rim0, rim1 = before(4 + b - 1), before(6 + b - 1)
        row0 = tap(0, b) * head0 + tap(1, b) * rim1 + tap(2, b) * rim0
        row1 = tap(0, b) * head1 + tap(1, b) * head0 + tap(2, b) * rim1
        starts = [row0, row1] if b == 1 else [starts[0] * row0, starts[1] * row1]
    start0, start1 = starts
    late0 = jnp.exp(-step * float(length - 1))
    late1 = jnp.exp(-step * float(length - 2))
    fade = jnp.exp(-step * float(length))
    incoming = jnp.zeros((modes, channels), jnp.float32)
    for j in range(seq_count):
        state = all_ref[j * ROWS : j * ROWS + modes, :]
        state = state + late0 * start0[j : j + 1, :] + late1 * start1[j : j + 1, :]
        incoming = jnp.where(j < me, incoming * fade + state, incoming)

    row = jax.lax.broadcasted_iota(jnp.int32, (TILE, channels), 0)
    mine0 = jnp.sum(jnp.where(order == me, start0, 0.0), axis=0, keepdims=True)
    mine1 = jnp.sum(jnp.where(order == me, start1, 0.0), axis=0, keepdims=True)
    rim0 = jnp.sum(jnp.where(order == me - 1, rows(8), 0.0), axis=0, keepdims=True)
    rim1 = jnp.sum(jnp.where(order == me - 1, rows(9), 0.0), axis=0, keepdims=True)
    extra0 = tap(1, 0) * rim1 + tap(2, 0) * rim0
    extra1 = tap(2, 0) * rim1

    lead = (row + 1).astype(jnp.float32)
    heads = []
    for m in range(modes):
        scale = gain_ref[m : m + 1, :] * incoming[m : m + 1, :]
        heads.append(scale * jnp.exp(-step[m : m + 1, :] * lead))
    skip = skip_ref[...]
    for q in range(tiles):
        at = slice(q * TILE, (q + 1) * TILE)
        value = conv_ref[at, :]
        value = value + mine0 * h_ref[(q + 1) * TILE : (q + 2) * TILE, :]
        value = value + mine1 * h_ref[(q + 1) * TILE - 1 : (q + 2) * TILE - 1, :]
        for m in range(modes):
            value = value + row_tile(e_ref, q * modes + m) * heads[m]
        gate = first_ref[at, :]
        if q == 0:
            value = value + jnp.where(row == 0, skip * mine0, jnp.where(row == 1, skip * mine1, 0.0))
            gate = gate + jnp.where(row == 0, extra0, jnp.where(row == 1, extra1, 0.0))
        value_ref[at, :] = gate * value
    out_ref[...] = value_ref[...].astype(out_ref.dtype)


def gather_features(features):
    shard_count = lax.axis_size("shard")
    line = shard_count // 2
    pairs = line // 2
    groups = [[l * line + 2 * q + p for q in range(pairs)] for l in range(2) for p in range(2)]
    across = [(i, (i + line) % shard_count) for i in range(shard_count)]
    up = [(l * line + z, l * line + (z - 1) % line) for l in range(2) for z in range(line)]
    down = [(l * line + z, l * line + (z + 1) % line) for l in range(2) for z in range(line)]
    few = 3 * pairs // 8

    near = lax.all_gather(features, "shard", axis=0, axis_index_groups=groups)
    far = lax.ppermute(near, "shard", across)
    odd = lax.ppermute(near, "shard", up)
    far_up = lax.ppermute(far[:few], "shard", up)
    far_down = lax.ppermute(far[few:], "shard", down)
    return near, odd, far, far_up, far_down


def shards(features, in_proj, short_filter, residue, decay_rate, skip_gain):
    length = features.shape[0]
    channels = in_proj.shape[2]
    modes = residue.shape[0]
    seq_count = lax.axis_size("seq")
    line = lax.axis_size("shard") // 2
    total = length * seq_count
    tiles = length // TILE
    f32 = jnp.float32
    vmem = pl.BlockSpec(memory_space=pltpu.VMEM)
    smem = pl.BlockSpec(memory_space=pltpu.SMEM)

    def params(mebibytes):
        return pltpu.CompilerParams(vmem_limit_bytes=mebibytes << 20)

    pieces = gather_features(features)
    w_branch = in_proj.transpose(1, 0, 2)
    at = lax.axis_index("shard")
    taps = lax.dynamic_slice_in_dim(short_filter, at * channels, channels, 2).reshape(-1, channels)
    h, e, gain = pl.pallas_call(
        functools.partial(tables_kernel, modes, length, total),
        out_shape=(
            jax.ShapeDtypeStruct((length + TILE, channels), f32),
            jax.ShapeDtypeStruct((tiles * modes, channels), f32),
            jax.ShapeDtypeStruct((modes, channels), f32),
        ),
        compiler_params=params(4),
        name="tables",
    )(decay_rate, residue)

    place = jnp.stack([at // line, at % 2]).astype(jnp.int32)
    near, odd, far, far_up, far_down = pieces
    early = pl.pallas_call(
        early_kernel,
        in_specs=[smem] + [vmem] * 4,
        out_specs=vmem,
        out_shape=jax.ShapeDtypeStruct((length, 3 * channels), f32),
        compiler_params=params(12),
        name="early",
    )(place, near, odd, far, w_branch)
    lead, drive, message = pl.pallas_call(
        functools.partial(project_kernel, modes, length, total),
        in_specs=[smem] + [vmem] * 7,
        out_specs=(vmem,) * 3,
        out_shape=(
            jax.ShapeDtypeStruct((length + TILE, channels), f32),
            jax.ShapeDtypeStruct((length, channels), f32),
            jax.ShapeDtypeStruct((seq_count, ROWS, channels), f32),
        ),
        scratch_shapes=[
            pltpu.VMEM((length + TILE, 2 * channels), f32),
            pltpu.VMEM((ROWS, channels), f32),
        ],
        compiler_params=params(12),
        name="project",
    )(place, early, far_up, far_down, w_branch, taps, decay_rate, e)

    everyone = lax.all_to_all(message, "seq", 0, 0).reshape(seq_count * ROWS, channels)
    skip = skip_gain.reshape(1, channels)
    conv, first = pl.pallas_call(
        functools.partial(conv_kernel, length),
        in_specs=[vmem] * 5,
        out_specs=(vmem,) * 2,
        out_shape=(jax.ShapeDtypeStruct((length, channels), f32),) * 2,
        scratch_shapes=[
            pltpu.VMEM((length + TILE, channels), f32),
            pltpu.VMEM((TILE, length, channels), f32),
        ],
        compiler_params=params(6),
        name="conv",
    )(drive, h, skip, lead, taps)

    me = lax.axis_index("seq").astype(jnp.int32).reshape(1)
    return pl.pallas_call(
        functools.partial(finish_kernel, modes, length, total, seq_count),
        in_specs=[smem] + [vmem] * 9,
        out_specs=vmem,
        out_shape=jax.ShapeDtypeStruct((length, channels), features.dtype),
        scratch_shapes=[pltpu.VMEM((length, channels), f32)],
        compiler_params=params(6),
        name="finish",
    )(me, everyone, first, conv, taps, decay_rate, gain, skip, h, e)


def solution(mesh):
    placed = (
        P("seq", "shard"),
        P(None, None, "shard"),
        P(),
        P(None, "shard"),
        P(None, "shard"),
        P("shard"),
    )
    return jax.shard_map(
        shards, mesh=mesh, in_specs=placed, out_specs=P("seq", "shard"), check_vma=False
    )
```

```python
import functools

import jax
import jax.numpy as jnp
from jax import lax
from jax.experimental import pallas as pl
from jax.experimental.pallas import tpu as pltpu
from jax.sharding import PartitionSpec as P

TILE = 8
ROWS = 32


def row_tile(ref, row):
    return jnp.broadcast_to(ref[row : row + 1, :], (TILE, ref.shape[1]))


def rise(z):
    value = jnp.full_like(z, 1.0 / 10.0)
    for n in range(9, 1, -1):
        value = (1.0 - z * value) * (1.0 / n)
    return z * (1.0 - z * value)


def tables_kernel(modes, length, total, rate_ref, residue_ref, h_ref, e_ref, gain_ref):
    tiles = length // TILE
    rate = rate_ref[...]
    step = rate * (1.0 / total)
    gain_ref[...] = residue_ref[...] * jnp.sqrt(rise(2.0 * step) / (1.0 - jnp.exp(-2.0 * rate)))
    lane = jax.lax.broadcasted_iota(jnp.int32, (TILE, step.shape[1]), 0).astype(jnp.float32)
    for q in range(tiles):
        e_ref[q * modes : (q + 1) * modes, :] = jnp.exp(-step * float(TILE * q))
    scaled = [gain_ref[m : m + 1, :] * jnp.exp(-step[m : m + 1, :] * lane) for m in range(modes)]
    h_ref[0:TILE, :] = jnp.zeros((TILE, step.shape[1]), jnp.float32)
    for q in range(tiles):
        total_tile = row_tile(e_ref, q * modes) * scaled[0]
        for m in range(1, modes):
            total_tile = total_tile + row_tile(e_ref, q * modes + m) * scaled[m]
        h_ref[(q + 1) * TILE : (q + 2) * TILE, :] = total_tile


def weight_rows(w_ref, owners, block):
    rows = []
    for owner in owners:
        at = pl.ds(pl.multiple_of(owner * block, block), block)
        rows.append(jnp.concatenate([w_ref[b, at, :] for b in range(3)], axis=1))
    return jnp.concatenate(rows, axis=0)


def early_kernel(place_ref, near_ref, odd_ref, far_ref, w_ref, acc_ref, rest_ref, held_ref, sems):
    line, parity = place_ref[0], place_ref[1]
    pairs, _, block = near_ref.shape
    steps = sems.shape[0]
    per_step = pairs // steps
    depth = 2 * per_step * block

    def copy(step, half):
        rows = pl.ds(half * 2 * pairs * block + step * depth, depth)
        return pltpu.make_async_copy(w_ref.at[:, rows, :], held_ref.at[:, rows, :], sems.at[step, half])

    for step in range(steps):
        for half in range(2):
            copy(step, half).start()
    for step in range(steps):
        for half in range(2):
            copy(step, half).wait()
        lefts, owners = [], []
        for i in range(step * per_step, (step + 1) * per_step):
            lefts += [near_ref[i], odd_ref[i], far_ref[i]]
            own, other = 2 * pairs * line + 2 * i, 2 * pairs * (1 - line) + 2 * i
            owners += [own + parity, own + 1 - parity, other + parity]
            rest_ref[i * block : (i + 1) * block, :] = weight_rows(held_ref, [other + 1 - parity], block)
        part = jnp.dot(
            jnp.concatenate(lefts, axis=1),
            weight_rows(held_ref, owners, block),
            preferred_element_type=jnp.float32,
        )
        acc_ref[...] = part if step == 0 else acc_ref[...] + part


def project_kernel(
    modes, length, total, early_ref, rest_ref, far_up_ref, far_down_ref, taps_ref, rate_ref,
    e_ref, lead_ref, drive_ref, message_ref, pair_ref, state_ref,
):
    channels = drive_ref.shape[1]
    left = [ref[k] for ref in (far_up_ref, far_down_ref) for k in range(ref.shape[0])]
    acc = early_ref[...] + jnp.dot(
        jnp.concatenate(left, axis=1), rest_ref[...], preferred_element_type=jnp.float32
    )
    proj = acc.astype(jnp.bfloat16).astype(jnp.float32)
    pad = TILE
    one, two, three = channels, 2 * channels, 3 * channels
    lead_ref[0:pad, :] = jnp.zeros((pad, channels), jnp.float32)
    lead_ref[pad:, :] = proj[:, 0:one]
    pair_ref[0:pad, :] = jnp.zeros((pad, two), jnp.float32)
    pair_ref[pad:, :] = proj[:, one:three]

    row = jax.lax.broadcasted_iota(jnp.int32, (TILE, channels), 0)
    taps = [[row_tile(taps_ref, 3 * j + b) for j in range(3)] for b in (1, 2)]
    tiles = length // TILE
    states = [None] * modes
    for q in range(tiles):
        drive = None
        for b in range(2):
            cols = slice(b * channels, (b + 1) * channels)
            at = pad + q * TILE
            value = taps[b][0] * pair_ref[at : at + TILE, cols]
            value = value + taps[b][1] * pair_ref[at - 1 : at - 1 + TILE, cols]
            value = value + taps[b][2] * pair_ref[at - 2 : at - 2 + TILE, cols]
            drive = value if b == 0 else drive * value
        if q == 0:
            drive = jnp.where(row < 2, 0.0, drive)
        drive_ref[q * TILE : (q + 1) * TILE, :] = drive
        for m in range(modes):
            term = row_tile(e_ref, (tiles - 1 - q) * modes + m) * drive
            states[m] = term if q == 0 else states[m] + term
    step = rate_ref[...] * (1.0 / total)
    lag = (TILE - 1 - row).astype(jnp.float32)
    for m in range(modes):
        state = states[m] * jnp.exp(-step[m : m + 1, :] * lag)
        state_ref[m : m + 1, :] = jnp.sum(state, axis=0, keepdims=True)
    head, tail = pad, pad + length - 2
    spots = [(r, b) for r in (head, head + 1, tail, tail + 1) for b in (0, 1)]
    for k, (r, b) in enumerate(spots):
        state_ref[modes + k : modes + k + 1, :] = pair_ref[r : r + 1, b * channels : (b + 1) * channels]
    used = modes + len(spots)
    state_ref[used : used + 2, :] = lead_ref[tail : tail + 2, :]
    state_ref[used + 2 : ROWS, :] = jnp.zeros((ROWS - used - 2, channels), jnp.float32)
    message = state_ref[...]
    for s in range(message_ref.shape[0]):
        message_ref[s] = message


def conv_kernel(length, drive_ref, h_ref, skip_ref, lead_ref, taps_ref, conv_ref, first_ref, pad_ref, lag_ref):
    channels = drive_ref.shape[1]
    tiles = length // TILE
    pad_ref[0:TILE, :] = jnp.zeros((TILE, channels), jnp.float32)
    pad_ref[TILE:, :] = drive_ref[...]
    for j in range(TILE):
        lag_ref[j] = pad_ref[TILE - j : TILE - j + length, :]

    for q in range(tiles):
        at = (q + 1) * TILE
        value = row_tile(taps_ref, 0) * lead_ref[at : at + TILE, :]
        value = value + row_tile(taps_ref, 3) * lead_ref[at - 1 : at - 1 + TILE, :]
        value = value + row_tile(taps_ref, 6) * lead_ref[at - 2 : at - 2 + TILE, :]
        first_ref[q * TILE : (q + 1) * TILE, :] = value

    group = 8
    for g in range(tiles // group):
        low = g * group

        def over_lags(j, accs):
            accs = list(accs)
            window = [lag_ref[j, pl.ds((low + i) * TILE, TILE), :] for i in range(group)]
            for p in range(low + group):
                weight = jnp.broadcast_to(h_ref[pl.ds(TILE * (p + 1) + j, 1), :], (TILE, channels))
                for i in range(group):
                    if low + i - p >= 0:
                        accs[i] = accs[i] + weight * window[i]
                below = low - p - 1
                fresh = lag_ref[j, pl.ds(below * TILE, TILE), :] if below >= 0 else None
                window = [fresh] + window[:-1]
            return tuple(accs)

        accs = tuple(skip_ref[...] * drive_ref[(low + i) * TILE : (low + i + 1) * TILE, :] for i in range(group))
        accs = lax.fori_loop(0, TILE, over_lags, accs)
        for i in range(group):
            conv_ref[(low + i) * TILE : (low + i + 1) * TILE, :] = accs[i]


def finish_kernel(
    modes, length, total, seq_count, me_ref, all_ref, first_ref, conv_ref, taps_ref, rate_ref,
    gain_ref, skip_ref, h_ref, e_ref, out_ref, value_ref,
):
    me = me_ref[0]
    channels = conv_ref.shape[1]
    tiles = length // TILE
    step = rate_ref[...] * (1.0 / total)

    def tap(j, b):
        return taps_ref[3 * j + b : 3 * j + b + 1, :]

    def rows(k):
        return all_ref[pl.ds(modes + k, seq_count, stride=ROWS), :]

    order = jax.lax.broadcasted_iota(jnp.int32, (seq_count, channels), 0)

    def before(k):
        return jnp.where(order == 0, 0.0, pltpu.roll(rows(k), 1, 0))

    starts = [None, None]
    for b in (1, 2):
        head0, head1 = rows(b - 1), rows(2 + b - 1)
        rim0, rim1 = before(4 + b - 1), before(6 + b - 1)
        row0 = tap(0, b) * head0 + tap(1, b) * rim1 + tap(2, b) * rim0
        row1 = tap(0, b) * head1 + tap(1, b) * head0 + tap(2, b) * rim1
        starts = [row0, row1] if b == 1 else [starts[0] * row0, starts[1] * row1]
    start0, start1 = starts
    late0 = jnp.exp(-step * float(length - 1))
    late1 = jnp.exp(-step * float(length - 2))
    fade = jnp.exp(-step * float(length))
    incoming = jnp.zeros((modes, channels), jnp.float32)
    for j in range(seq_count):
        state = all_ref[j * ROWS : j * ROWS + modes, :]
        state = state + late0 * start0[j : j + 1, :] + late1 * start1[j : j + 1, :]
        incoming = jnp.where(j < me, incoming * fade + state, incoming)

    row = jax.lax.broadcasted_iota(jnp.int32, (TILE, channels), 0)
    mine0 = jnp.sum(jnp.where(order == me, start0, 0.0), axis=0, keepdims=True)
    mine1 = jnp.sum(jnp.where(order == me, start1, 0.0), axis=0, keepdims=True)
    rim0 = jnp.sum(jnp.where(order == me - 1, rows(8), 0.0), axis=0, keepdims=True)
    rim1 = jnp.sum(jnp.where(order == me - 1, rows(9), 0.0), axis=0, keepdims=True)
    extra0 = tap(1, 0) * rim1 + tap(2, 0) * rim0
    extra1 = tap(2, 0) * rim1

    lead = (row + 1).astype(jnp.float32)
    heads = []
    for m in range(modes):
        scale = gain_ref[m : m + 1, :] * incoming[m : m + 1, :]
        heads.append(scale * jnp.exp(-step[m : m + 1, :] * lead))
    skip = skip_ref[...]
    for q in range(tiles):
        at = slice(q * TILE, (q + 1) * TILE)
        value = conv_ref[at, :]
        value = value + mine0 * h_ref[(q + 1) * TILE : (q + 2) * TILE, :]
        value = value + mine1 * h_ref[(q + 1) * TILE - 1 : (q + 2) * TILE - 1, :]
        for m in range(modes):
            value = value + row_tile(e_ref, q * modes + m) * heads[m]
        gate = first_ref[at, :]
        if q == 0:
            value = value + jnp.where(row == 0, skip * mine0, jnp.where(row == 1, skip * mine1, 0.0))
            gate = gate + jnp.where(row == 0, extra0, jnp.where(row == 1, extra1, 0.0))
        value_ref[at, :] = gate * value
    out_ref[...] = value_ref[...].astype(out_ref.dtype)


def gather_features(features, *ready):
    shard_count = lax.axis_size("shard")
    line = shard_count // 2
    pairs = line // 2
    groups = [[l * line + 2 * q + p for q in range(pairs)] for l in range(2) for p in range(2)]
    across = [(i, (i + line) % shard_count) for i in range(shard_count)]
    up = [(l * line + z, l * line + (z - 1) % line) for l in range(2) for z in range(line)]
    down = [(l * line + z, l * line + (z + 1) % line) for l in range(2) for z in range(line)]
    few = 3 * pairs // 8

    near = lax.all_gather(features, "shard", axis=0, axis_index_groups=groups)
    far = lax.ppermute(near, "shard", across)
    odd = lax.ppermute(near, "shard", up)
    far, *ready = lax.optimization_barrier((far, *ready))
    far_up = lax.ppermute(far[:few], "shard", up)
    far_down = lax.ppermute(far[few:], "shard", down)
    return (near, odd, far, far_up, far_down), ready


def shards(features, in_proj, short_filter, residue, decay_rate, skip_gain):
    length = features.shape[0]
    channels = in_proj.shape[2]
    modes = residue.shape[0]
    seq_count = lax.axis_size("seq")
    line = lax.axis_size("shard") // 2
    total = length * seq_count
    tiles = length // TILE
    f32 = jnp.float32
    vmem = pl.BlockSpec(memory_space=pltpu.VMEM)
    smem = pl.BlockSpec(memory_space=pltpu.SMEM)

    def params(mebibytes):
        return pltpu.CompilerParams(vmem_limit_bytes=mebibytes << 20)

    w_branch = in_proj.transpose(1, 0, 2)
    at = lax.axis_index("shard")
    taps = lax.dynamic_slice_in_dim(short_filter, at * channels, channels, 2).reshape(-1, channels)
    tables = pl.pallas_call(
        functools.partial(tables_kernel, modes, length, total),
        out_shape=(
            jax.ShapeDtypeStruct((length + TILE, channels), f32),
            jax.ShapeDtypeStruct((tiles * modes, channels), f32),
            jax.ShapeDtypeStruct((modes, channels), f32),
        ),
        compiler_params=params(4),
        name="tables",
    )(decay_rate, residue)

    pieces, (h, e, gain) = gather_features(features, *tables)
    place = jnp.stack([at // line, at % 2]).astype(jnp.int32)
    near, odd, far, far_up, far_down = pieces
    hbm = pl.BlockSpec(memory_space=pltpu.HBM)
    pairs, _, block = near.shape
    early, rest = pl.pallas_call(
        early_kernel,
        in_specs=[smem] + [vmem] * 3 + [hbm],
        out_specs=(vmem,) * 2,
        out_shape=(
            jax.ShapeDtypeStruct((length, 3 * channels), f32),
            jax.ShapeDtypeStruct((pairs * block, 3 * channels), w_branch.dtype),
        ),
        scratch_shapes=[
            pltpu.VMEM(w_branch.shape, w_branch.dtype),
            pltpu.SemaphoreType.DMA((pairs // 2, 2)),
        ],
        compiler_params=params(14),
        name="early",
    )(place, near, odd, far, pltpu.with_memory_space_constraint(w_branch, pltpu.HBM))
    lead, drive, message = pl.pallas_call(
        functools.partial(project_kernel, modes, length, total),
        in_specs=[vmem] * 7,
        out_specs=(vmem,) * 3,
        out_shape=(
            jax.ShapeDtypeStruct((length + TILE, channels), f32),
            jax.ShapeDtypeStruct((length, channels), f32),
            jax.ShapeDtypeStruct((seq_count, ROWS, channels), f32),
        ),
        scratch_shapes=[
            pltpu.VMEM((length + TILE, 2 * channels), f32),
            pltpu.VMEM((ROWS, channels), f32),
        ],
        compiler_params=params(12),
        name="project",
    )(early, rest, far_up, far_down, taps, decay_rate, e)

    everyone = lax.all_to_all(message, "seq", 0, 0).reshape(seq_count * ROWS, channels)
    skip = skip_gain.reshape(1, channels)
    conv, first = pl.pallas_call(
        functools.partial(conv_kernel, length),
        in_specs=[vmem] * 5,
        out_specs=(vmem,) * 2,
        out_shape=(jax.ShapeDtypeStruct((length, channels), f32),) * 2,
        scratch_shapes=[
            pltpu.VMEM((length + TILE, channels), f32),
            pltpu.VMEM((TILE, length, channels), f32),
        ],
        compiler_params=params(6),
        name="conv",
    )(drive, h, skip, lead, taps)

    me = lax.axis_index("seq").astype(jnp.int32).reshape(1)
    return pl.pallas_call(
        functools.partial(finish_kernel, modes, length, total, seq_count),
        in_specs=[smem] + [vmem] * 9,
        out_specs=vmem,
        out_shape=jax.ShapeDtypeStruct((length, channels), features.dtype),
        scratch_shapes=[pltpu.VMEM((length, channels), f32)],
        compiler_params=params(6),
        name="finish",
    )(me, everyone, first, conv, taps, decay_rate, gain, skip, h, e)


def solution(mesh):
    placed = (
        P("seq", "shard"),
        P(None, None, "shard"),
        P(),
        P(None, "shard"),
        P(None, "shard"),
        P("shard"),
    )
    return jax.shard_map(
        shards, mesh=mesh, in_specs=placed, out_specs=P("seq", "shard"), check_vma=False
    )
```

```python
import functools

import jax
import jax.numpy as jnp
from jax import lax
from jax.experimental import pallas as pl
from jax.experimental.pallas import tpu as pltpu
from jax.sharding import PartitionSpec as P

TILE = 8
ROWS = 32


def row_tile(ref, row):
    return jnp.broadcast_to(ref[row : row + 1, :], (TILE, ref.shape[1]))


def rise(z):
    value = jnp.full_like(z, 1.0 / 10.0)
    for n in range(9, 1, -1):
        value = (1.0 - z * value) * (1.0 / n)
    return z * (1.0 - z * value)


def tables_kernel(modes, length, total, rate_ref, residue_ref, h_ref, e_ref, gain_ref):
    tiles = length // TILE
    rate = rate_ref[...]
    step = rate * (1.0 / total)
    gain_ref[...] = residue_ref[...] * jnp.sqrt(rise(2.0 * step) / (1.0 - jnp.exp(-2.0 * rate)))
    lane = jax.lax.broadcasted_iota(jnp.int32, (TILE, step.shape[1]), 0).astype(jnp.float32)
    for q in range(tiles):
        e_ref[q * modes : (q + 1) * modes, :] = jnp.exp(-step * float(TILE * q))
    scaled = [gain_ref[m : m + 1, :] * jnp.exp(-step[m : m + 1, :] * lane) for m in range(modes)]
    h_ref[0:TILE, :] = jnp.zeros((TILE, step.shape[1]), jnp.float32)
    for q in range(tiles):
        total_tile = row_tile(e_ref, q * modes) * scaled[0]
        for m in range(1, modes):
            total_tile = total_tile + row_tile(e_ref, q * modes + m) * scaled[m]
        h_ref[(q + 1) * TILE : (q + 2) * TILE, :] = total_tile


def side_by_side(held_ref, starts, block):
    rows = []
    for start in starts:
        at = pl.ds(start, block)
        rows.append(jnp.concatenate([held_ref[b, at, :] for b in range(3)], axis=1))
    return jnp.concatenate(rows, axis=0)


def first_kernel(place_ref, near_ref, w_ref, acc_ref, held_ref, sems):
    line, parity = place_ref[0], place_ref[1]
    pairs, _, block = near_ref.shape

    def copy(i):
        owner = 2 * pairs * line + 2 * i + parity
        rows = pl.ds(pl.multiple_of(owner * block, block), block)
        return pltpu.make_async_copy(w_ref.at[:, rows, :], held_ref.at[:, pl.ds(i * block, block), :], sems.at[i])

    for i in range(pairs):
        copy(i).start()
    for i in range(0, pairs, 4):
        for k in range(i, i + 4):
            copy(k).wait()
        part = jnp.dot(
            jnp.concatenate([near_ref[k] for k in range(i, i + 4)], axis=1),
            side_by_side(held_ref, [k * block for k in range(i, i + 4)], block),
            preferred_element_type=jnp.float32,
        )
        acc_ref[...] = part if i == 0 else acc_ref[...] + part


def early_kernel(place_ref, first_ref, odd_ref, far_ref, w_ref, acc_ref, rest_ref, held_ref, sems):
    line, parity = place_ref[0], place_ref[1]
    pairs, _, block = odd_ref.shape

    def copies(i):
        own = 2 * pairs * line + 2 * i + 1 - parity
        other = 2 * pairs * (1 - line) + 2 * i
        one = pl.ds(pl.multiple_of(own * block, block), block)
        two = pl.ds(pl.multiple_of(other * block, block), 2 * block)
        at = 3 * i * block
        return (
            pltpu.make_async_copy(w_ref.at[:, one, :], held_ref.at[:, pl.ds(at, block), :], sems.at[i, 0]),
            pltpu.make_async_copy(
                w_ref.at[:, two, :], held_ref.at[:, pl.ds(at + block, 2 * block), :], sems.at[i, 1]
            ),
        )

    for i in range(pairs):
        for copy in copies(i):
            copy.start()
    for i in range(0, pairs, 2):
        lefts, starts = [], []
        for k in (i, i + 1):
            for copy in copies(k):
                copy.wait()
            at = 3 * k * block
            same = pl.multiple_of(at + block + parity * block, block)
            cross = pl.multiple_of(at + 2 * block - parity * block, block)
            lefts += [odd_ref[k], far_ref[k]]
            starts += [at, same]
            rest_ref[k * block : (k + 1) * block, :] = side_by_side(held_ref, [cross], block)
        part = jnp.dot(
            jnp.concatenate(lefts, axis=1),
            side_by_side(held_ref, starts, block),
            preferred_element_type=jnp.float32,
        )
        acc_ref[...] = (first_ref[...] if i == 0 else acc_ref[...]) + part


def project_kernel(
    modes, length, total, early_ref, rest_ref, far_up_ref, far_down_ref, taps_ref, rate_ref,
    e_ref, lead_ref, drive_ref, message_ref, pair_ref, state_ref,
):
    channels = drive_ref.shape[1]
    left = [ref[k] for ref in (far_up_ref, far_down_ref) for k in range(ref.shape[0])]
    acc = early_ref[...] + jnp.dot(
        jnp.concatenate(left, axis=1), rest_ref[...], preferred_element_type=jnp.float32
    )
    proj = acc.astype(jnp.bfloat16).astype(jnp.float32)
    pad = TILE
    one, two, three = channels, 2 * channels, 3 * channels
    lead_ref[0:pad, :] = jnp.zeros((pad, channels), jnp.float32)
    lead_ref[pad:, :] = proj[:, 0:one]
    pair_ref[0:pad, :] = jnp.zeros((pad, two), jnp.float32)
    pair_ref[pad:, :] = proj[:, one:three]

    row = jax.lax.broadcasted_iota(jnp.int32, (TILE, channels), 0)
    taps = [[row_tile(taps_ref, 3 * j + b) for j in range(3)] for b in (1, 2)]
    tiles = length // TILE
    states = [None] * modes
    for q in range(tiles):
        drive = None
        for b in range(2):
            cols = slice(b * channels, (b + 1) * channels)
            at = pad + q * TILE
            value = taps[b][0] * pair_ref[at : at + TILE, cols]
            value = value + taps[b][1] * pair_ref[at - 1 : at - 1 + TILE, cols]
            value = value + taps[b][2] * pair_ref[at - 2 : at - 2 + TILE, cols]
            drive = value if b == 0 else drive * value
        if q == 0:
            drive = jnp.where(row < 2, 0.0, drive)
        drive_ref[q * TILE : (q + 1) * TILE, :] = drive
        for m in range(modes):
            term = row_tile(e_ref, (tiles - 1 - q) * modes + m) * drive
            states[m] = term if q == 0 else states[m] + term
    step = rate_ref[...] * (1.0 / total)
    lag = (TILE - 1 - row).astype(jnp.float32)
    for m in range(modes):
        state = states[m] * jnp.exp(-step[m : m + 1, :] * lag)
        state_ref[m : m + 1, :] = jnp.sum(state, axis=0, keepdims=True)
    head, tail = pad, pad + length - 2
    spots = [(r, b) for r in (head, head + 1, tail, tail + 1) for b in (0, 1)]
    for k, (r, b) in enumerate(spots):
        state_ref[modes + k : modes + k + 1, :] = pair_ref[r : r + 1, b * channels : (b + 1) * channels]
    used = modes + len(spots)
    state_ref[used : used + 2, :] = lead_ref[tail : tail + 2, :]
    state_ref[used + 2 : ROWS, :] = jnp.zeros((ROWS - used - 2, channels), jnp.float32)
    message = state_ref[...]
    for s in range(message_ref.shape[0]):
        message_ref[s] = message


def conv_kernel(length, drive_ref, h_ref, skip_ref, lead_ref, taps_ref, conv_ref, first_ref, pad_ref, lag_ref):
    channels = drive_ref.shape[1]
    tiles = length // TILE
    pad_ref[0:TILE, :] = jnp.zeros((TILE, channels), jnp.float32)
    pad_ref[TILE:, :] = drive_ref[...]
    for j in range(TILE):
        lag_ref[j] = pad_ref[TILE - j : TILE - j + length, :]

    for q in range(tiles):
        at = (q + 1) * TILE
        value = row_tile(taps_ref, 0) * lead_ref[at : at + TILE, :]
        value = value + row_tile(taps_ref, 3) * lead_ref[at - 1 : at - 1 + TILE, :]
        value = value + row_tile(taps_ref, 6) * lead_ref[at - 2 : at - 2 + TILE, :]
        first_ref[q * TILE : (q + 1) * TILE, :] = value

    group = 8
    for g in range(tiles // group):
        low = g * group

        def over_lags(j, accs):
            accs = list(accs)
            window = [lag_ref[j, pl.ds((low + i) * TILE, TILE), :] for i in range(group)]
            for p in range(low + group):
                weight = jnp.broadcast_to(h_ref[pl.ds(TILE * (p + 1) + j, 1), :], (TILE, channels))
                for i in range(group):
                    if low + i - p >= 0:
                        accs[i] = accs[i] + weight * window[i]
                below = low - p - 1
                fresh = lag_ref[j, pl.ds(below * TILE, TILE), :] if below >= 0 else None
                window = [fresh] + window[:-1]
            return tuple(accs)

        accs = tuple(skip_ref[...] * drive_ref[(low + i) * TILE : (low + i + 1) * TILE, :] for i in range(group))
        accs = lax.fori_loop(0, TILE, over_lags, accs)
        for i in range(group):
            conv_ref[(low + i) * TILE : (low + i + 1) * TILE, :] = accs[i]


def finish_kernel(
    modes, length, total, seq_count, me_ref, all_ref, first_ref, conv_ref, taps_ref, rate_ref,
    gain_ref, skip_ref, h_ref, e_ref, out_ref, value_ref,
):
    me = me_ref[0]
    channels = conv_ref.shape[1]
    tiles = length // TILE
    step = rate_ref[...] * (1.0 / total)

    def tap(j, b):
        return taps_ref[3 * j + b : 3 * j + b + 1, :]

    def rows(k):
        return all_ref[pl.ds(modes + k, seq_count, stride=ROWS), :]

    order = jax.lax.broadcasted_iota(jnp.int32, (seq_count, channels), 0)

    def before(k):
        return jnp.where(order == 0, 0.0, pltpu.roll(rows(k), 1, 0))

    starts = [None, None]
    for b in (1, 2):
        head0, head1 = rows(b - 1), rows(2 + b - 1)
        rim0, rim1 = before(4 + b - 1), before(6 + b - 1)
        row0 = tap(0, b) * head0 + tap(1, b) * rim1 + tap(2, b) * rim0
        row1 = tap(0, b) * head1 + tap(1, b) * head0 + tap(2, b) * rim1
        starts = [row0, row1] if b == 1 else [starts[0] * row0, starts[1] * row1]
    start0, start1 = starts
    late0 = jnp.exp(-step * float(length - 1))
    late1 = jnp.exp(-step * float(length - 2))
    fade = jnp.exp(-step * float(length))
    incoming = jnp.zeros((modes, channels), jnp.float32)
    for j in range(seq_count):
        state = all_ref[j * ROWS : j * ROWS + modes, :]
        state = state + late0 * start0[j : j + 1, :] + late1 * start1[j : j + 1, :]
        incoming = jnp.where(j < me, incoming * fade + state, incoming)

    row = jax.lax.broadcasted_iota(jnp.int32, (TILE, channels), 0)
    mine0 = jnp.sum(jnp.where(order == me, start0, 0.0), axis=0, keepdims=True)
    mine1 = jnp.sum(jnp.where(order == me, start1, 0.0), axis=0, keepdims=True)
    rim0 = jnp.sum(jnp.where(order == me - 1, rows(8), 0.0), axis=0, keepdims=True)
    rim1 = jnp.sum(jnp.where(order == me - 1, rows(9), 0.0), axis=0, keepdims=True)
    extra0 = tap(1, 0) * rim1 + tap(2, 0) * rim0
    extra1 = tap(2, 0) * rim1

    lead = (row + 1).astype(jnp.float32)
    heads = []
    for m in range(modes):
        scale = gain_ref[m : m + 1, :] * incoming[m : m + 1, :]
        heads.append(scale * jnp.exp(-step[m : m + 1, :] * lead))
    skip = skip_ref[...]
    for q in range(tiles):
        at = slice(q * TILE, (q + 1) * TILE)
        value = conv_ref[at, :]
        value = value + mine0 * h_ref[(q + 1) * TILE : (q + 2) * TILE, :]
        value = value + mine1 * h_ref[(q + 1) * TILE - 1 : (q + 2) * TILE - 1, :]
        for m in range(modes):
            value = value + row_tile(e_ref, q * modes + m) * heads[m]
        gate = first_ref[at, :]
        if q == 0:
            value = value + jnp.where(row == 0, skip * mine0, jnp.where(row == 1, skip * mine1, 0.0))
            gate = gate + jnp.where(row == 0, extra0, jnp.where(row == 1, extra1, 0.0))
        value_ref[at, :] = gate * value
    out_ref[...] = value_ref[...].astype(out_ref.dtype)


def gather_features(features, prepare):
    shard_count = lax.axis_size("shard")
    line = shard_count // 2
    pairs = line // 2
    groups = [[l * line + 2 * q + p for q in range(pairs)] for l in range(2) for p in range(2)]
    across = [(i, (i + line) % shard_count) for i in range(shard_count)]
    up = [(l * line + z, l * line + (z - 1) % line) for l in range(2) for z in range(line)]
    down = [(l * line + z, l * line + (z + 1) % line) for l in range(2) for z in range(line)]
    few = 3 * pairs // 8

    near = lax.all_gather(features, "shard", axis=0, axis_index_groups=groups)
    ready = prepare(near)
    far = lax.ppermute(near, "shard", across)
    odd = lax.ppermute(near, "shard", up)
    far, *ready = lax.optimization_barrier((far, *ready))
    far_up = lax.ppermute(far[:few], "shard", up)
    far_down = lax.ppermute(far[few:], "shard", down)
    return (odd, far, far_up, far_down), ready


def shards(features, in_proj, short_filter, residue, decay_rate, skip_gain):
    length = features.shape[0]
    channels = in_proj.shape[2]
    modes = residue.shape[0]
    seq_count = lax.axis_size("seq")
    line = lax.axis_size("shard") // 2
    total = length * seq_count
    tiles = length // TILE
    f32 = jnp.float32
    vmem = pl.BlockSpec(memory_space=pltpu.VMEM)
    smem = pl.BlockSpec(memory_space=pltpu.SMEM)

    def params(mebibytes):
        return pltpu.CompilerParams(vmem_limit_bytes=mebibytes << 20)

    w_branch = in_proj.transpose(1, 0, 2)
    at = lax.axis_index("shard")
    taps = lax.dynamic_slice_in_dim(short_filter, at * channels, channels, 2).reshape(-1, channels)
    tables = pl.pallas_call(
        functools.partial(tables_kernel, modes, length, total),
        out_shape=(
            jax.ShapeDtypeStruct((length + TILE, channels), f32),
            jax.ShapeDtypeStruct((tiles * modes, channels), f32),
            jax.ShapeDtypeStruct((modes, channels), f32),
        ),
        compiler_params=params(4),
        name="tables",
    )(decay_rate, residue)

    place = jnp.stack([at // line, at % 2]).astype(jnp.int32)
    hbm = pl.BlockSpec(memory_space=pltpu.HBM)
    pairs, block = line // 2, features.shape[1]
    total_shape = jax.ShapeDtypeStruct((length, 3 * channels), f32)
    w_far = pltpu.with_memory_space_constraint(w_branch, pltpu.HBM)

    def prepare(near):
        begun = pl.pallas_call(
            first_kernel,
            in_specs=[smem, vmem, hbm],
            out_specs=vmem,
            out_shape=total_shape,
            scratch_shapes=[
                pltpu.VMEM((3, pairs * block, channels), w_branch.dtype),
                pltpu.SemaphoreType.DMA((pairs,)),
            ],
            compiler_params=params(8),
            name="begin",
        )(place, near, w_far)
        return (begun, *tables)

    pieces, (begun, h, e, gain) = gather_features(features, prepare)
    odd, far, far_up, far_down = pieces
    early, rest = pl.pallas_call(
        early_kernel,
        in_specs=[smem] + [vmem] * 3 + [hbm],
        out_specs=(vmem,) * 2,
        out_shape=(
            total_shape,
            jax.ShapeDtypeStruct((pairs * block, 3 * channels), w_branch.dtype),
        ),
        scratch_shapes=[
            pltpu.VMEM((3, 3 * pairs * block, channels), w_branch.dtype),
            pltpu.SemaphoreType.DMA((pairs, 2)),
        ],
        compiler_params=params(12),
        name="early",
    )(place, begun, odd, far, w_far)
    lead, drive, message = pl.pallas_call(
        functools.partial(project_kernel, modes, length, total),
        in_specs=[vmem] * 7,
        out_specs=(vmem,) * 3,
        out_shape=(
            jax.ShapeDtypeStruct((length + TILE, channels), f32),
            jax.ShapeDtypeStruct((length, channels), f32),
            jax.ShapeDtypeStruct((seq_count, ROWS, channels), f32),
        ),
        scratch_shapes=[
            pltpu.VMEM((length + TILE, 2 * channels), f32),
            pltpu.VMEM((ROWS, channels), f32),
        ],
        compiler_params=params(12),
        name="project",
    )(early, rest, far_up, far_down, taps, decay_rate, e)

    everyone = lax.all_to_all(message, "seq", 0, 0).reshape(seq_count * ROWS, channels)
    skip = skip_gain.reshape(1, channels)
    conv, first = pl.pallas_call(
        functools.partial(conv_kernel, length),
        in_specs=[vmem] * 5,
        out_specs=(vmem,) * 2,
        out_shape=(jax.ShapeDtypeStruct((length, channels), f32),) * 2,
        scratch_shapes=[
            pltpu.VMEM((length + TILE, channels), f32),
            pltpu.VMEM((TILE, length, channels), f32),
        ],
        compiler_params=params(6),
        name="conv",
    )(drive, h, skip, lead, taps)

    me = lax.axis_index("seq").astype(jnp.int32).reshape(1)
    return pl.pallas_call(
        functools.partial(finish_kernel, modes, length, total, seq_count),
        in_specs=[smem] + [vmem] * 9,
        out_specs=vmem,
        out_shape=jax.ShapeDtypeStruct((length, channels), features.dtype),
        scratch_shapes=[pltpu.VMEM((length, channels), f32)],
        compiler_params=params(6),
        name="finish",
    )(me, everyone, first, conv, taps, decay_rate, gain, skip, h, e)


def solution(mesh):
    placed = (
        P("seq", "shard"),
        P(None, None, "shard"),
        P(),
        P(None, "shard"),
        P(None, "shard"),
        P("shard"),
    )
    return jax.shard_map(
        shards, mesh=mesh, in_specs=placed, out_specs=P("seq", "shard"), check_vma=False
    )
```

```python
import functools

import jax
import jax.numpy as jnp
from jax import lax
from jax.experimental import pallas as pl
from jax.experimental.pallas import tpu as pltpu
from jax.sharding import PartitionSpec as P

TILE = 8
ROWS = 32


def row_tile(ref, row):
    return jnp.broadcast_to(ref[row : row + 1, :], (TILE, ref.shape[1]))


def rise(z):
    value = jnp.full_like(z, 1.0 / 10.0)
    for n in range(9, 1, -1):
        value = (1.0 - z * value) * (1.0 / n)
    return z * (1.0 - z * value)


def tables(modes, length, total, rate_ref, residue_ref, h_ref, e_ref, gain_ref):
    tiles = length // TILE
    rate = rate_ref[...]
    step = rate * (1.0 / total)
    gain_ref[...] = residue_ref[...] * jnp.sqrt(rise(2.0 * step) / (1.0 - jnp.exp(-2.0 * rate)))
    lane = jax.lax.broadcasted_iota(jnp.int32, (TILE, step.shape[1]), 0).astype(jnp.float32)
    for q in range(tiles):
        e_ref[q * modes : (q + 1) * modes, :] = jnp.exp(-step * float(TILE * q))
    scaled = [gain_ref[m : m + 1, :] * jnp.exp(-step[m : m + 1, :] * lane) for m in range(modes)]
    h_ref[0:TILE, :] = jnp.zeros((TILE, step.shape[1]), jnp.float32)
    for q in range(tiles):
        total_tile = row_tile(e_ref, q * modes) * scaled[0]
        for m in range(1, modes):
            total_tile = total_tile + row_tile(e_ref, q * modes + m) * scaled[m]
        h_ref[(q + 1) * TILE : (q + 2) * TILE, :] = total_tile


def weight_rows(w_ref, owners, block):
    rows = []
    for owner in owners:
        at = pl.ds(pl.multiple_of(owner * block, block), block)
        rows.append(jnp.concatenate([w_ref[b, at, :] for b in range(3)], axis=1))
    return jnp.concatenate(rows, axis=0)


def early_kernel(
    modes, length, total, place_ref, near_ref, odd_ref, far_low_ref, far_high_ref, rate_ref, residue_ref,
    w_ref, acc_ref, rest_ref, h_ref, e_ref, gain_ref, held_ref, modes_ref, sems, mode_sems,
):
    line, parity = place_ref[0], place_ref[1]
    pairs, _, block = near_ref.shape
    few = far_low_ref.shape[0]
    steps = sems.shape[0]
    per_step = pairs // steps
    depth = 2 * per_step * block

    def copy(step, half):
        rows = pl.ds(half * 2 * pairs * block + step * depth, depth)
        return pltpu.make_async_copy(w_ref.at[:, rows, :], held_ref.at[:, rows, :], sems.at[step, half])

    small = [
        pltpu.make_async_copy(ref, modes_ref.at[k], mode_sems.at[k])
        for k, ref in enumerate((rate_ref, residue_ref))
    ]
    for each in small:
        each.start()
    for step in range(steps):
        for half in range(2):
            copy(step, half).start()
    for each in small:
        each.wait()
    tables(modes, length, total, modes_ref.at[0], modes_ref.at[1], h_ref, e_ref, gain_ref)
    for step in range(steps):
        for half in range(2):
            copy(step, half).wait()
        lefts, owners = [], []
        for i in range(step * per_step, (step + 1) * per_step):
            lefts += [near_ref[i], odd_ref[i], far_low_ref[i] if i < few else far_high_ref[i - few]]
            own, other = 2 * pairs * line + 2 * i, 2 * pairs * (1 - line) + 2 * i
            owners += [own + parity, own + 1 - parity, other + parity]
            rest_ref[i * block : (i + 1) * block, :] = weight_rows(held_ref, [other + 1 - parity], block)
        part = jnp.dot(
            jnp.concatenate(lefts, axis=1),
            weight_rows(held_ref, owners, block),
            preferred_element_type=jnp.float32,
        )
        acc_ref[...] = part if step == 0 else acc_ref[...] + part


def project_kernel(
    modes, length, total, early_ref, rest_ref, far_up_ref, far_down_ref, taps_ref, rate_ref,
    e_ref, lead_ref, drive_ref, message_ref, pair_ref, state_ref,
):
    channels = drive_ref.shape[1]
    left = [ref[k] for ref in (far_up_ref, far_down_ref) for k in range(ref.shape[0])]
    acc = early_ref[...] + jnp.dot(
        jnp.concatenate(left, axis=1), rest_ref[...], preferred_element_type=jnp.float32
    )
    proj = acc.astype(jnp.bfloat16).astype(jnp.float32)
    pad = TILE
    one, two, three = channels, 2 * channels, 3 * channels
    lead_ref[0:pad, :] = jnp.zeros((pad, channels), jnp.float32)
    lead_ref[pad:, :] = proj[:, 0:one]
    pair_ref[0:pad, :] = jnp.zeros((pad, two), jnp.float32)
    pair_ref[pad:, :] = proj[:, one:three]

    row = jax.lax.broadcasted_iota(jnp.int32, (TILE, channels), 0)
    taps = [[row_tile(taps_ref, 3 * j + b) for j in range(3)] for b in (1, 2)]
    tiles = length // TILE
    states = [None] * modes
    for q in range(tiles):
        drive = None
        for b in range(2):
            cols = slice(b * channels, (b + 1) * channels)
            at = pad + q * TILE
            value = taps[b][0] * pair_ref[at : at + TILE, cols]
            value = value + taps[b][1] * pair_ref[at - 1 : at - 1 + TILE, cols]
            value = value + taps[b][2] * pair_ref[at - 2 : at - 2 + TILE, cols]
            drive = value if b == 0 else drive * value
        if q == 0:
            drive = jnp.where(row < 2, 0.0, drive)
        drive_ref[q * TILE : (q + 1) * TILE, :] = drive
        for m in range(modes):
            term = row_tile(e_ref, (tiles - 1 - q) * modes + m) * drive
            states[m] = term if q == 0 else states[m] + term
    step = rate_ref[...] * (1.0 / total)
    lag = (TILE - 1 - row).astype(jnp.float32)
    for m in range(modes):
        state = states[m] * jnp.exp(-step[m : m + 1, :] * lag)
        state_ref[m : m + 1, :] = jnp.sum(state, axis=0, keepdims=True)
    head, tail = pad, pad + length - 2
    spots = [(r, b) for r in (head, head + 1, tail, tail + 1) for b in (0, 1)]
    for k, (r, b) in enumerate(spots):
        state_ref[modes + k : modes + k + 1, :] = pair_ref[r : r + 1, b * channels : (b + 1) * channels]
    used = modes + len(spots)
    state_ref[used : used + 2, :] = lead_ref[tail : tail + 2, :]
    state_ref[used + 2 : ROWS, :] = jnp.zeros((ROWS - used - 2, channels), jnp.float32)
    message = state_ref[...]
    for s in range(message_ref.shape[0]):
        message_ref[s] = message


def conv_kernel(length, drive_ref, h_ref, skip_ref, lead_ref, taps_ref, conv_ref, first_ref, pad_ref, lag_ref):
    channels = drive_ref.shape[1]
    tiles = length // TILE
    pad_ref[0:TILE, :] = jnp.zeros((TILE, channels), jnp.float32)
    pad_ref[TILE:, :] = drive_ref[...]
    for j in range(TILE):
        lag_ref[j] = pad_ref[TILE - j : TILE - j + length, :]

    for q in range(tiles):
        at = (q + 1) * TILE
        value = row_tile(taps_ref, 0) * lead_ref[at : at + TILE, :]
        value = value + row_tile(taps_ref, 3) * lead_ref[at - 1 : at - 1 + TILE, :]
        value = value + row_tile(taps_ref, 6) * lead_ref[at - 2 : at - 2 + TILE, :]
        first_ref[q * TILE : (q + 1) * TILE, :] = value

    group = 8
    for g in range(tiles // group):
        low = g * group

        def over_lags(j, accs):
            accs = list(accs)
            window = [lag_ref[j, pl.ds((low + i) * TILE, TILE), :] for i in range(group)]
            for p in range(low + group):
                weight = jnp.broadcast_to(h_ref[pl.ds(TILE * (p + 1) + j, 1), :], (TILE, channels))
                for i in range(group):
                    if low + i - p >= 0:
                        accs[i] = accs[i] + weight * window[i]
                below = low - p - 1
                fresh = lag_ref[j, pl.ds(below * TILE, TILE), :] if below >= 0 else None
                window = [fresh] + window[:-1]
            return tuple(accs)

        accs = tuple(skip_ref[...] * drive_ref[(low + i) * TILE : (low + i + 1) * TILE, :] for i in range(group))
        accs = lax.fori_loop(0, TILE, over_lags, accs)
        for i in range(group):
            conv_ref[(low + i) * TILE : (low + i + 1) * TILE, :] = accs[i]


def finish_kernel(
    modes, length, total, seq_count, me_ref, all_ref, first_ref, conv_ref, taps_ref, rate_ref,
    gain_ref, skip_ref, h_ref, e_ref, out_ref, value_ref,
):
    me = me_ref[0]
    channels = conv_ref.shape[1]
    tiles = length // TILE
    step = rate_ref[...] * (1.0 / total)

    def tap(j, b):
        return taps_ref[3 * j + b : 3 * j + b + 1, :]

    def rows(k):
        return all_ref[pl.ds(modes + k, seq_count, stride=ROWS), :]

    order = jax.lax.broadcasted_iota(jnp.int32, (seq_count, channels), 0)

    def before(k):
        return jnp.where(order == 0, 0.0, pltpu.roll(rows(k), 1, 0))

    starts = [None, None]
    for b in (1, 2):
        head0, head1 = rows(b - 1), rows(2 + b - 1)
        rim0, rim1 = before(4 + b - 1), before(6 + b - 1)
        row0 = tap(0, b) * head0 + tap(1, b) * rim1 + tap(2, b) * rim0
        row1 = tap(0, b) * head1 + tap(1, b) * head0 + tap(2, b) * rim1
        starts = [row0, row1] if b == 1 else [starts[0] * row0, starts[1] * row1]
    start0, start1 = starts
    late0 = jnp.exp(-step * float(length - 1))
    late1 = jnp.exp(-step * float(length - 2))
    fade = jnp.exp(-step * float(length))
    incoming = jnp.zeros((modes, channels), jnp.float32)
    for j in range(seq_count):
        state = all_ref[j * ROWS : j * ROWS + modes, :]
        state = state + late0 * start0[j : j + 1, :] + late1 * start1[j : j + 1, :]
        incoming = jnp.where(j < me, incoming * fade + state, incoming)

    row = jax.lax.broadcasted_iota(jnp.int32, (TILE, channels), 0)
    mine0 = jnp.sum(jnp.where(order == me, start0, 0.0), axis=0, keepdims=True)
    mine1 = jnp.sum(jnp.where(order == me, start1, 0.0), axis=0, keepdims=True)
    rim0 = jnp.sum(jnp.where(order == me - 1, rows(8), 0.0), axis=0, keepdims=True)
    rim1 = jnp.sum(jnp.where(order == me - 1, rows(9), 0.0), axis=0, keepdims=True)
    extra0 = tap(1, 0) * rim1 + tap(2, 0) * rim0
    extra1 = tap(2, 0) * rim1

    lead = (row + 1).astype(jnp.float32)
    heads = []
    for m in range(modes):
        scale = gain_ref[m : m + 1, :] * incoming[m : m + 1, :]
        heads.append(scale * jnp.exp(-step[m : m + 1, :] * lead))
    skip = skip_ref[...]
    for q in range(tiles):
        at = slice(q * TILE, (q + 1) * TILE)
        value = conv_ref[at, :]
        value = value + mine0 * h_ref[(q + 1) * TILE : (q + 2) * TILE, :]
        value = value + mine1 * h_ref[(q + 1) * TILE - 1 : (q + 2) * TILE - 1, :]
        for m in range(modes):
            value = value + row_tile(e_ref, q * modes + m) * heads[m]
        gate = first_ref[at, :]
        if q == 0:
            value = value + jnp.where(row == 0, skip * mine0, jnp.where(row == 1, skip * mine1, 0.0))
            gate = gate + jnp.where(row == 0, extra0, jnp.where(row == 1, extra1, 0.0))
        value_ref[at, :] = gate * value
    out_ref[...] = value_ref[...].astype(out_ref.dtype)


def gather_features(features):
    shard_count = lax.axis_size("shard")
    line = shard_count // 2
    pairs = line // 2
    groups = [[l * line + 2 * q + p for q in range(pairs)] for l in range(2) for p in range(2)]
    across = [(i, (i + line) % shard_count) for i in range(shard_count)]
    up = [(l * line + z, l * line + (z - 1) % line) for l in range(2) for z in range(line)]
    down = [(l * line + z, l * line + (z + 1) % line) for l in range(2) for z in range(line)]
    few = 3 * pairs // 8

    near = lax.all_gather(features, "shard", axis=0, axis_index_groups=groups)
    far_high = lax.ppermute(near[few:], "shard", across)
    odd = lax.ppermute(near, "shard", up)
    far_low = lax.ppermute(near[:few], "shard", across)
    far_down = lax.ppermute(far_high, "shard", down)
    far_up = lax.ppermute(far_low, "shard", up)
    return near, odd, far_low, far_high, far_up, far_down


def shards(features, in_proj, short_filter, residue, decay_rate, skip_gain):
    length = features.shape[0]
    channels = in_proj.shape[2]
    modes = residue.shape[0]
    seq_count = lax.axis_size("seq")
    line = lax.axis_size("shard") // 2
    total = length * seq_count
    tiles = length // TILE
    f32 = jnp.float32
    vmem = pl.BlockSpec(memory_space=pltpu.VMEM)
    smem = pl.BlockSpec(memory_space=pltpu.SMEM)

    def params(mebibytes):
        return pltpu.CompilerParams(vmem_limit_bytes=mebibytes << 20)

    w_branch = in_proj.transpose(1, 0, 2)
    at = lax.axis_index("shard")
    taps = lax.dynamic_slice_in_dim(short_filter, at * channels, channels, 2).reshape(-1, channels)
    place = jnp.stack([at // line, at % 2]).astype(jnp.int32)
    near, odd, far_low, far_high, far_up, far_down = gather_features(features)
    hbm = pl.BlockSpec(memory_space=pltpu.HBM)
    pairs, _, block = near.shape
    early, rest, h, e, gain = pl.pallas_call(
        functools.partial(early_kernel, modes, length, total),
        in_specs=[smem] + [vmem] * 4 + [hbm] * 3,
        out_specs=(vmem,) * 5,
        out_shape=(
            jax.ShapeDtypeStruct((length, 3 * channels), f32),
            jax.ShapeDtypeStruct((pairs * block, 3 * channels), w_branch.dtype),
            jax.ShapeDtypeStruct((length + TILE, channels), f32),
            jax.ShapeDtypeStruct((tiles * modes, channels), f32),
            jax.ShapeDtypeStruct((modes, channels), f32),
        ),
        scratch_shapes=[
            pltpu.VMEM(w_branch.shape, w_branch.dtype),
            pltpu.VMEM((2, modes, channels), f32),
            pltpu.SemaphoreType.DMA((pairs // 2, 2)),
            pltpu.SemaphoreType.DMA((2,)),
        ],
        compiler_params=params(14),
        name="early",
    )(place, near, odd, far_low, far_high, *(pltpu.with_memory_space_constraint(a, pltpu.HBM) for a in (decay_rate, residue, w_branch)))
    lead, drive, message = pl.pallas_call(
        functools.partial(project_kernel, modes, length, total),
        in_specs=[vmem] * 7,
        out_specs=(vmem,) * 3,
        out_shape=(
            jax.ShapeDtypeStruct((length + TILE, channels), f32),
            jax.ShapeDtypeStruct((length, channels), f32),
            jax.ShapeDtypeStruct((seq_count, ROWS, channels), f32),
        ),
        scratch_shapes=[
            pltpu.VMEM((length + TILE, 2 * channels), f32),
            pltpu.VMEM((ROWS, channels), f32),
        ],
        compiler_params=params(12),
        name="project",
    )(early, rest, far_up, far_down, taps, decay_rate, e)

    everyone = lax.all_to_all(message, "seq", 0, 0).reshape(seq_count * ROWS, channels)
    skip = skip_gain.reshape(1, channels)
    conv, first = pl.pallas_call(
        functools.partial(conv_kernel, length),
        in_specs=[vmem] * 5,
        out_specs=(vmem,) * 2,
        out_shape=(jax.ShapeDtypeStruct((length, channels), f32),) * 2,
        scratch_shapes=[
            pltpu.VMEM((length + TILE, channels), f32),
            pltpu.VMEM((TILE, length, channels), f32),
        ],
        compiler_params=params(6),
        name="conv",
    )(drive, h, skip, lead, taps)

    me = lax.axis_index("seq").astype(jnp.int32).reshape(1)
    return pl.pallas_call(
        functools.partial(finish_kernel, modes, length, total, seq_count),
        in_specs=[smem] + [vmem] * 9,
        out_specs=vmem,
        out_shape=jax.ShapeDtypeStruct((length, channels), features.dtype),
        scratch_shapes=[pltpu.VMEM((length, channels), f32)],
        compiler_params=params(6),
        name="finish",
    )(me, everyone, first, conv, taps, decay_rate, gain, skip, h, e)


def solution(mesh):
    placed = (
        P("seq", "shard"),
        P(None, None, "shard"),
        P(),
        P(None, "shard"),
        P(None, "shard"),
        P("shard"),
    )
    return jax.shard_map(
        shards, mesh=mesh, in_specs=placed, out_specs=P("seq", "shard"), check_vma=False
    )
```

```python
import functools

import jax
import jax.numpy as jnp
from jax import lax
from jax.experimental import pallas as pl
from jax.experimental.pallas import tpu as pltpu
from jax.sharding import PartitionSpec as P

TILE = 8
ROWS = 32


def row_tile(ref, row):
    return jnp.broadcast_to(ref[row : row + 1, :], (TILE, ref.shape[1]))


def rise(z):
    value = jnp.full_like(z, 1.0 / 10.0)
    for n in range(9, 1, -1):
        value = (1.0 - z * value) * (1.0 / n)
    return z * (1.0 - z * value)


def tables_kernel(modes, length, total, rate_ref, residue_ref, h_ref, e_ref, gain_ref):
    tiles = length // TILE
    rate = rate_ref[...]
    step = rate * (1.0 / total)
    gain_ref[...] = residue_ref[...] * jnp.sqrt(rise(2.0 * step) / (1.0 - jnp.exp(-2.0 * rate)))
    lane = jax.lax.broadcasted_iota(jnp.int32, (TILE, step.shape[1]), 0).astype(jnp.float32)
    for q in range(tiles):
        e_ref[q * modes : (q + 1) * modes, :] = jnp.exp(-step * float(TILE * q))
    scaled = [gain_ref[m : m + 1, :] * jnp.exp(-step[m : m + 1, :] * lane) for m in range(modes)]
    h_ref[0:TILE, :] = jnp.zeros((TILE, step.shape[1]), jnp.float32)
    for q in range(tiles):
        total_tile = row_tile(e_ref, q * modes) * scaled[0]
        for m in range(1, modes):
            total_tile = total_tile + row_tile(e_ref, q * modes + m) * scaled[m]
        h_ref[(q + 1) * TILE : (q + 2) * TILE, :] = total_tile


def weight_rows(w_ref, owners, block):
    rows = []
    for owner in owners:
        at = pl.ds(pl.multiple_of(owner * block, block), block)
        rows.append(jnp.concatenate([w_ref[b, at, :] for b in range(3)], axis=1))
    return jnp.concatenate(rows, axis=0)


def early_kernel(place_ref, near_ref, odd_ref, far_ref, w_ref, acc_ref, rest_ref, held_ref, sems):
    line, parity = place_ref[0], place_ref[1]
    pairs, _, block = near_ref.shape
    steps = sems.shape[0]
    per_step = pairs // steps
    depth = 2 * per_step * block

    def copy(step, half):
        rows = pl.ds(half * 2 * pairs * block + step * depth, depth)
        return pltpu.make_async_copy(w_ref.at[:, rows, :], held_ref.at[:, rows, :], sems.at[step, half])

    for step in range(steps):
        for half in range(2):
            copy(step, half).start()
    for step in range(steps):
        for half in range(2):
            copy(step, half).wait()
        lefts, owners = [], []
        for i in range(step * per_step, (step + 1) * per_step):
            lefts += [near_ref[i], odd_ref[i], far_ref[i]]
            own, other = 2 * pairs * line + 2 * i, 2 * pairs * (1 - line) + 2 * i
            owners += [own + parity, own + 1 - parity, other + parity]
            rest_ref[i * block : (i + 1) * block, :] = weight_rows(held_ref, [other + 1 - parity], block)
        part = jnp.dot(
            jnp.concatenate(lefts, axis=1),
            weight_rows(held_ref, owners, block),
            preferred_element_type=jnp.float32,
        )
        acc_ref[...] = part if step == 0 else acc_ref[...] + part


def project_kernel(
    modes, length, total, early_ref, rest_ref, far_up_ref, far_down_ref, taps_ref, rate_ref,
    e_ref, lead_ref, drive_ref, message_ref, pair_ref, state_ref,
):
    channels = drive_ref.shape[1]
    left = [ref[k] for ref in (far_up_ref, far_down_ref) for k in range(ref.shape[0])]
    acc = early_ref[...] + jnp.dot(
        jnp.concatenate(left, axis=1), rest_ref[...], preferred_element_type=jnp.float32
    )
    proj = acc.astype(jnp.bfloat16).astype(jnp.float32)
    pad = TILE
    one, two, three = channels, 2 * channels, 3 * channels
    lead_ref[0:pad, :] = jnp.zeros((pad, channels), jnp.float32)
    lead_ref[pad:, :] = proj[:, 0:one]
    pair_ref[0:pad, :] = jnp.zeros((pad, two), jnp.float32)
    pair_ref[pad:, :] = proj[:, one:three]

    row = jax.lax.broadcasted_iota(jnp.int32, (TILE, channels), 0)
    taps = [[row_tile(taps_ref, 3 * j + b) for j in range(3)] for b in (1, 2)]
    tiles = length // TILE
    states = [None] * modes
    for q in range(tiles):
        drive = None
        for b in range(2):
            cols = slice(b * channels, (b + 1) * channels)
            at = pad + q * TILE
            value = taps[b][0] * pair_ref[at : at + TILE, cols]
            value = value + taps[b][1] * pair_ref[at - 1 : at - 1 + TILE, cols]
            value = value + taps[b][2] * pair_ref[at - 2 : at - 2 + TILE, cols]
            drive = value if b == 0 else drive * value
        if q == 0:
            drive = jnp.where(row < 2, 0.0, drive)
        drive_ref[q * TILE : (q + 1) * TILE, :] = drive
        for m in range(modes):
            term = row_tile(e_ref, (tiles - 1 - q) * modes + m) * drive
            states[m] = term if q == 0 else states[m] + term
    step = rate_ref[...] * (1.0 / total)
    lag = (TILE - 1 - row).astype(jnp.float32)
    for m in range(modes):
        state = states[m] * jnp.exp(-step[m : m + 1, :] * lag)
        state_ref[m : m + 1, :] = jnp.sum(state, axis=0, keepdims=True)
    head, tail = pad, pad + length - 2
    spots = [(r, b) for r in (head, head + 1, tail, tail + 1) for b in (0, 1)]
    for k, (r, b) in enumerate(spots):
        state_ref[modes + k : modes + k + 1, :] = pair_ref[r : r + 1, b * channels : (b + 1) * channels]
    used = modes + len(spots)
    state_ref[used : used + 2, :] = lead_ref[tail : tail + 2, :]
    state_ref[used + 2 : ROWS, :] = jnp.zeros((ROWS - used - 2, channels), jnp.float32)
    message = state_ref[...]
    for s in range(message_ref.shape[0]):
        message_ref[s] = message


def conv_kernel(length, drive_ref, h_ref, skip_ref, lead_ref, taps_ref, conv_ref, first_ref, pad_ref, lag_ref):
    channels = drive_ref.shape[1]
    tiles = length // TILE
    pad_ref[0:TILE, :] = jnp.zeros((TILE, channels), jnp.float32)
    pad_ref[TILE:, :] = drive_ref[...]
    for j in range(TILE):
        lag_ref[j] = pad_ref[TILE - j : TILE - j + length, :]

    for q in range(tiles):
        at = (q + 1) * TILE
        value = row_tile(taps_ref, 0) * lead_ref[at : at + TILE, :]
        value = value + row_tile(taps_ref, 3) * lead_ref[at - 1 : at - 1 + TILE, :]
        value = value + row_tile(taps_ref, 6) * lead_ref[at - 2 : at - 2 + TILE, :]
        first_ref[q * TILE : (q + 1) * TILE, :] = value

    group = 8
    for g in range(tiles // group):
        low = g * group

        def over_lags(j, accs):
            accs = list(accs)
            window = [lag_ref[j, pl.ds((low + i) * TILE, TILE), :] for i in range(group)]
            for p in range(low + group):
                weight = jnp.broadcast_to(h_ref[pl.ds(TILE * (p + 1) + j, 1), :], (TILE, channels))
                for i in range(group):
                    if low + i - p >= 0:
                        accs[i] = accs[i] + weight * window[i]
                below = low - p - 1
                fresh = lag_ref[j, pl.ds(below * TILE, TILE), :] if below >= 0 else None
                window = [fresh] + window[:-1]
            return tuple(accs)

        accs = tuple(skip_ref[...] * drive_ref[(low + i) * TILE : (low + i + 1) * TILE, :] for i in range(group))
        accs = lax.fori_loop(0, TILE, over_lags, accs)
        for i in range(group):
            conv_ref[(low + i) * TILE : (low + i + 1) * TILE, :] = accs[i]


def finish_kernel(
    modes, length, total, seq_count, me_ref, all_ref, first_ref, conv_ref, taps_ref, rate_ref,
    gain_ref, skip_ref, h_ref, e_ref, out_ref, value_ref,
):
    me = me_ref[0]
    channels = conv_ref.shape[1]
    tiles = length // TILE
    step = rate_ref[...] * (1.0 / total)

    def tap(j, b):
        return taps_ref[3 * j + b : 3 * j + b + 1, :]

    def rows(k):
        return all_ref[pl.ds(modes + k, seq_count, stride=ROWS), :]

    order = jax.lax.broadcasted_iota(jnp.int32, (seq_count, channels), 0)

    def before(k):
        return jnp.where(order == 0, 0.0, pltpu.roll(rows(k), 1, 0))

    starts = [None, None]
    for b in (1, 2):
        head0, head1 = rows(b - 1), rows(2 + b - 1)
        rim0, rim1 = before(4 + b - 1), before(6 + b - 1)
        row0 = tap(0, b) * head0 + tap(1, b) * rim1 + tap(2, b) * rim0
        row1 = tap(0, b) * head1 + tap(1, b) * head0 + tap(2, b) * rim1
        starts = [row0, row1] if b == 1 else [starts[0] * row0, starts[1] * row1]
    start0, start1 = starts
    late0 = jnp.exp(-step * float(length - 1))
    late1 = jnp.exp(-step * float(length - 2))
    fade = jnp.exp(-step * float(length))
    incoming = jnp.zeros((modes, channels), jnp.float32)
    for j in range(seq_count):
        state = all_ref[j * ROWS : j * ROWS + modes, :]
        state = state + late0 * start0[j : j + 1, :] + late1 * start1[j : j + 1, :]
        incoming = jnp.where(j < me, incoming * fade + state, incoming)

    row = jax.lax.broadcasted_iota(jnp.int32, (TILE, channels), 0)
    mine0 = jnp.sum(jnp.where(order == me, start0, 0.0), axis=0, keepdims=True)
    mine1 = jnp.sum(jnp.where(order == me, start1, 0.0), axis=0, keepdims=True)
    rim0 = jnp.sum(jnp.where(order == me - 1, rows(8), 0.0), axis=0, keepdims=True)
    rim1 = jnp.sum(jnp.where(order == me - 1, rows(9), 0.0), axis=0, keepdims=True)
    extra0 = tap(1, 0) * rim1 + tap(2, 0) * rim0
    extra1 = tap(2, 0) * rim1

    lead = (row + 1).astype(jnp.float32)
    heads = []
    for m in range(modes):
        scale = gain_ref[m : m + 1, :] * incoming[m : m + 1, :]
        heads.append(scale * jnp.exp(-step[m : m + 1, :] * lead))
    skip = skip_ref[...]
    for q in range(tiles):
        at = slice(q * TILE, (q + 1) * TILE)
        value = conv_ref[at, :]
        value = value + mine0 * h_ref[(q + 1) * TILE : (q + 2) * TILE, :]
        value = value + mine1 * h_ref[(q + 1) * TILE - 1 : (q + 2) * TILE - 1, :]
        for m in range(modes):
            value = value + row_tile(e_ref, q * modes + m) * heads[m]
        gate = first_ref[at, :]
        if q == 0:
            value = value + jnp.where(row == 0, skip * mine0, jnp.where(row == 1, skip * mine1, 0.0))
            gate = gate + jnp.where(row == 0, extra0, jnp.where(row == 1, extra1, 0.0))
        value_ref[at, :] = gate * value
    out_ref[...] = value_ref[...].astype(out_ref.dtype)


def gather_features(features, *ready):
    shard_count = lax.axis_size("shard")
    line = shard_count // 2
    pairs = line // 2
    groups = [[l * line + 2 * q + p for q in range(pairs)] for l in range(2) for p in range(2)]
    across = [(i, (i + line) % shard_count) for i in range(shard_count)]
    up = [(l * line + z, l * line + (z - 1) % line) for l in range(2) for z in range(line)]
    down = [(l * line + z, l * line + (z + 1) % line) for l in range(2) for z in range(line)]
    few = 3 * pairs // 8

    near = lax.all_gather(features, "shard", axis=0, axis_index_groups=groups)
    far = lax.ppermute(near, "shard", across)
    odd = lax.ppermute(near, "shard", up)
    far, *ready = lax.optimization_barrier((far, *ready))
    far_up = lax.ppermute(far[:few], "shard", up)
    far_down = lax.ppermute(far[few:], "shard", down)
    return (near, odd, far, far_up, far_down), ready


def shards(features, in_proj, short_filter, residue, decay_rate, skip_gain):
    length = features.shape[0]
    channels = in_proj.shape[2]
    modes = residue.shape[0]
    seq_count = lax.axis_size("seq")
    line = lax.axis_size("shard") // 2
    total = length * seq_count
    tiles = length // TILE
    f32 = jnp.float32
    vmem = pl.BlockSpec(memory_space=pltpu.VMEM)
    smem = pl.BlockSpec(memory_space=pltpu.SMEM)

    def params(mebibytes):
        return pltpu.CompilerParams(vmem_limit_bytes=mebibytes << 20)

    w_branch = in_proj.transpose(1, 0, 2)
    at = lax.axis_index("shard")
    taps = lax.dynamic_slice_in_dim(short_filter, at * channels, channels, 2).reshape(-1, channels)
    tables = pl.pallas_call(
        functools.partial(tables_kernel, modes, length, total),
        out_shape=(
            jax.ShapeDtypeStruct((length + TILE, channels), f32),
            jax.ShapeDtypeStruct((tiles * modes, channels), f32),
            jax.ShapeDtypeStruct((modes, channels), f32),
        ),
        compiler_params=params(4),
        name="tables",
    )(decay_rate, residue)

    pieces, (h, e, gain) = gather_features(features, *tables)
    place = jnp.stack([at // line, at % 2]).astype(jnp.int32)
    near, odd, far, far_up, far_down = pieces
    hbm = pl.BlockSpec(memory_space=pltpu.HBM)
    pairs, _, block = near.shape
    early, rest = pl.pallas_call(
        early_kernel,
        in_specs=[smem] + [vmem] * 3 + [hbm],
        out_specs=(vmem,) * 2,
        out_shape=(
            jax.ShapeDtypeStruct((length, 3 * channels), f32),
            jax.ShapeDtypeStruct((pairs * block, 3 * channels), w_branch.dtype),
        ),
        scratch_shapes=[
            pltpu.VMEM(w_branch.shape, w_branch.dtype),
            pltpu.SemaphoreType.DMA((pairs, 2)),
        ],
        compiler_params=params(14),
        name="early",
    )(place, near, odd, far, pltpu.with_memory_space_constraint(w_branch, pltpu.HBM))
    lead, drive, message = pl.pallas_call(
        functools.partial(project_kernel, modes, length, total),
        in_specs=[vmem] * 7,
        out_specs=(vmem,) * 3,
        out_shape=(
            jax.ShapeDtypeStruct((length + TILE, channels), f32),
            jax.ShapeDtypeStruct((length, channels), f32),
            jax.ShapeDtypeStruct((seq_count, ROWS, channels), f32),
        ),
        scratch_shapes=[
            pltpu.VMEM((length + TILE, 2 * channels), f32),
            pltpu.VMEM((ROWS, channels), f32),
        ],
        compiler_params=params(12),
        name="project",
    )(early, rest, far_up, far_down, taps, decay_rate, e)

    everyone = lax.all_to_all(message, "seq", 0, 0).reshape(seq_count * ROWS, channels)
    skip = skip_gain.reshape(1, channels)
    conv, first = pl.pallas_call(
        functools.partial(conv_kernel, length),
        in_specs=[vmem] * 5,
        out_specs=(vmem,) * 2,
        out_shape=(jax.ShapeDtypeStruct((length, channels), f32),) * 2,
        scratch_shapes=[
            pltpu.VMEM((length + TILE, channels), f32),
            pltpu.VMEM((TILE, length, channels), f32),
        ],
        compiler_params=params(6),
        name="conv",
    )(drive, h, skip, lead, taps)

    me = lax.axis_index("seq").astype(jnp.int32).reshape(1)
    return pl.pallas_call(
        functools.partial(finish_kernel, modes, length, total, seq_count),
        in_specs=[smem] + [vmem] * 9,
        out_specs=vmem,
        out_shape=jax.ShapeDtypeStruct((length, channels), features.dtype),
        scratch_shapes=[pltpu.VMEM((length, channels), f32)],
        compiler_params=params(6),
        name="finish",
    )(me, everyone, first, conv, taps, decay_rate, gain, skip, h, e)


def solution(mesh):
    placed = (
        P("seq", "shard"),
        P(None, None, "shard"),
        P(),
        P(None, "shard"),
        P(None, "shard"),
        P("shard"),
    )
    return jax.shard_map(
        shards, mesh=mesh, in_specs=placed, out_specs=P("seq", "shard"), check_vma=False
    )
```
